768 devices in a mesh: gx: 96 (over y, z), gy: 8 (over x, core).
Axes of the slice: x: 4, y: 8, z: 12, core: 2. Of those that a mesh axis runs over, the one named last changes fastest.
Arguments:
- component_share_field: float32 [32, 768, 64, 128], P(None, 'gx', 'gy'), may hold values from 0.05 to 1
- scaled_heat_level: float32 [768, 64, 128], P('gx', 'gy'), may hold values from 1 to 2.5
- local_transport_value: float32 [768, 64, 128], P('gx', 'gy'), may hold values from 0.5 to 2
- component_spreading_scale: float32 [16], replicated, may hold values from 0.1 to 1
- screened_poisson_reactive_term: float32 [16], replicated, may hold values from 0.5 to 4
- expansion_contribution_scale: float32 [32], replicated, may hold values from -3 to 3
- logarithm_arrhenius_constant: float32 [128], replicated, may hold values from -3 to -1
- arrhenius_energy_scale: float32 [128], replicated, may hold values from 0 to 4
- kinetic_exponents: int32 [128, 32], replicated, may hold values 0 or 1
- reaction_change_matrix: int32 [32, 128], replicated, may hold values from -1 to 1
Outputs:
- species_new: float32 [16, 768, 64, 128], P(None, 'gx', 'gy')
- div_field: float32 [768, 64, 128], P('gx', 'gy')
The draws below stay inside these ranges and needn't reach their ends.
Inputs may be any that keep to these rules, and one draw needn't show every extreme that they name: `reaction_change_matrix`: each entry is -1, 0 or 1.
All inputs are finite; a program needn't handle non-finite values.
Results may differ from the reference program's by a relative error of at most 0.0001.
Values sent between devices are 32-bit elements; how exact they have to be, the bound alone decides.
A program may use at most 32 MiB of HBM per device.

```python
import math
import jax
import jax.numpy as jnp
import numpy as np
from jax import lax

NSPEC = 32
NSOLVE = 16
REACT = 128
ITERS = 2
POINTS_ALONG_X = 768
POINTS_ALONG_Y = 64
POINTS_ALONG_Z = 128


def set_ends(entries, stream_key, low, high):
    longest = entries.shape.index(max(entries.shape))
    spots = []
    for shift in (0, 1):
        where = [jax.random.randint(jax.random.fold_in(stream_key, axis), (), 0, length) for axis, length in enumerate(entries.shape)]
        where[longest] = (where[longest] + shift) % entries.shape[longest]
        spots.append(tuple(where))
    return entries.at[spots[0]].set(low).at[spots[1]].set(high)


def block_scale(stream_key, dims, cuts, low, high):
    gain, own = 1.0, jax.random.fold_in(stream_key, 6)
    for position, blocks in cuts:
        draws = jnp.exp(jax.random.uniform(jax.random.fold_in(own, position), (blocks,), jnp.float32, low / len(cuts), high / len(cuts)))
        gain = gain * jnp.repeat(draws, dims[position] // blocks).reshape([-1 if axis == position else 1 for axis in range(len(dims))])
    return gain


def centred(rng, dims, scale, most, kind=jnp.bfloat16):
    values = scale * jax.random.normal(rng, dims, jnp.float32)
    return jnp.clip(values, min=-most, max=most).astype(kind)


def setup_inputs(seed: int = 0) -> dict:
    streams_of = jax.random.split(jax.random.key(seed), 11)
    return {
        "component_share_field": jnp.clip(jnp.exp(math.log(1.0) - 2.9957323 * jax.random.uniform(streams_of[0], (NSPEC, POINTS_ALONG_X, POINTS_ALONG_Y, POINTS_ALONG_Z), jnp.float32) ** block_scale(streams_of[0], (NSPEC, POINTS_ALONG_X, POINTS_ALONG_Y, POINTS_ALONG_Z), ((1, 96), (2, 8)), -0.2, 0.2)), 0.05, 1.0),
        "scaled_heat_level": jnp.clip(1.0 + 1.5 * jax.random.uniform(streams_of[1], (POINTS_ALONG_X, POINTS_ALONG_Y, POINTS_ALONG_Z), jnp.float32) ** block_scale(streams_of[1], (POINTS_ALONG_X, POINTS_ALONG_Y, POINTS_ALONG_Z), ((0, 96), (1, 8)), -0.2, 0.2), 1.0, 2.5),
        "local_transport_value": jnp.clip(jnp.exp(math.log(2.0) - 1.3862944 * jax.random.uniform(streams_of[2], (POINTS_ALONG_X, POINTS_ALONG_Y, POINTS_ALONG_Z), jnp.float32) ** block_scale(streams_of[2], (POINTS_ALONG_X, POINTS_ALONG_Y, POINTS_ALONG_Z), ((0, 96), (1, 8)), -0.2, 0.2)), 0.5, 2.0),
        "component_spreading_scale": jnp.clip(jnp.exp(jax.random.uniform(streams_of[3], (NSOLVE,), jnp.float32, math.log(0.1), math.log(1.0))), 0.1, 1.0),
        "screened_poisson_reactive_term": jnp.clip(jnp.exp(jax.random.uniform(streams_of[4], (NSOLVE,), jnp.float32, math.log(0.5), math.log(4.0))), 0.5, 4.0),
        "expansion_contribution_scale": centred(streams_of[5], (NSPEC,), 0.5, 3.0, jnp.float32),
        "logarithm_arrhenius_constant": jnp.clip(jax.random.uniform(streams_of[6], (REACT,), jnp.float32, -3.0, -1.0), -3.0, -1.0),
        "arrhenius_energy_scale": jnp.clip(jax.random.uniform(streams_of[7], (REACT,), jnp.float32, 0.0, 4.0), 0.0, 4.0),
        "kinetic_exponents": set_ends((jax.random.randint(streams_of[8], (REACT, NSPEC), 0, 16) < 1).astype(jnp.int32), jax.random.fold_in(streams_of[8], 1), 0, 1),
        "reaction_change_matrix": set_ends(jax.random.randint(streams_of[9], (NSPEC, REACT), -1, 2), jax.random.fold_in(streams_of[9], 1), -1, 1).astype(jnp.int32),
    }


def legendre_seven(points):
    return (429.0 * points ** 7 - 693.0 * points ** 5 + 315.0 * points ** 3 - 35.0 * points) / 16.0


def gll_tables():
    gll_nodes = np.array([-1.0, -0.8717401485096066, -0.5917001814331423, -0.2092992179024789, 0.2092992179024789, 0.5917001814331423, 0.8717401485096066, 1.0])
    at_nodes = legendre_seven(gll_nodes)
    weights = 2.0 / (56.0 * at_nodes * at_nodes)
    derivative = np.zeros((8, 8))
    for row_index in range(8):
        for col_index in range(8):
            if row_index != col_index:
                derivative[row_index, col_index] = at_nodes[row_index] / (at_nodes[col_index] * (gll_nodes[row_index] - gll_nodes[col_index]))
    derivative[0, 0] = -14.0
    derivative[7, 7] = 14.0
    return derivative, weights


def mass_weights(size_x, size_y, size_z, weights):
    table = jnp.asarray(weights, jnp.float32)
    along_one = jnp.tile(table, size_x // 8)
    along_two = jnp.tile(table, size_y // 8)
    along_three = jnp.tile(table, size_z // 8)
    return along_one[:, None, None] * along_two[None, :, None] * along_three[None, None, :]


def multiplicities(size_x, size_y, size_z):
    table = jnp.asarray(np.array([2.0, 1, 1, 1, 1, 1, 1, 2.0]), jnp.float32)
    along_one = jnp.tile(table, size_x // 8)
    along_two = jnp.tile(table, size_y // 8)
    along_three = jnp.tile(table, size_z // 8)
    return along_one[:, None, None] * along_two[None, :, None] * along_three[None, None, :]


def along_x(values, matrix):
    count_s, size_x, size_y, size_z = values.shape
    blocks = values.reshape(count_s, size_x // 8, 8, size_y, size_z)
    result = jnp.einsum("ij,aejyz->aeiyz", matrix, blocks, precision=lax.Precision.HIGHEST)
    return result.reshape(count_s, size_x, size_y, size_z)


def along_y(values, matrix):
    count_s, size_x, size_y, size_z = values.shape
    blocks = values.reshape(count_s, size_x, size_y // 8, 8, size_z)
    result = jnp.einsum("ij,axejz->axeiz", matrix, blocks, precision=lax.Precision.HIGHEST)
    return result.reshape(count_s, size_x, size_y, size_z)


def along_z(values, matrix):
    size_z = values.shape[3]
    block_deriv = jnp.kron(jnp.eye(size_z // 8, dtype=jnp.float32), matrix)
    return jnp.dot(values, block_deriv.T, precision=lax.Precision.HIGHEST)


def stiffness(values, weighted_cond, deriv_mat):
    trans_mat = deriv_mat.T
    stiff_sum = along_x(weighted_cond * along_x(values, deriv_mat), trans_mat)
    stiff_sum = stiff_sum + along_y(weighted_cond * along_y(values, deriv_mat), trans_mat)
    return stiff_sum + along_z(weighted_cond * along_z(values, deriv_mat), trans_mat)


def diag_stiffness(weighted_cond, deriv_mat):
    square_t = (deriv_mat * deriv_mat).T
    source = weighted_cond[None]
    return along_x(source, square_t) + along_y(source, square_t) + along_z(source, square_t)


def reaction_speeds(fractions, temps, kinetic_exponents_float, change_matrix_float, logarithm_arrhenius_constant, arrhenius_energy_scale):
    species_all = fractions.shape[0]
    log_frac = jnp.log(fractions).reshape(species_all, -1)
    exponent = jnp.dot(kinetic_exponents_float, log_frac, precision=lax.Precision.HIGHEST) + logarithm_arrhenius_constant[:, None] - arrhenius_energy_scale[:, None] * (1.0 / temps.reshape(1, -1) - 1.0)
    progress = jnp.exp(exponent)
    return jnp.dot(change_matrix_float, progress, precision=lax.Precision.HIGHEST).reshape(fractions.shape)


def shared_sum(values):
    for which_dim in (1, 2, 3):
        length = values.shape[which_dim]
        node_pos = jnp.arange(length) % 8
        shape_b = [1, 1, 1, 1]
        shape_b[which_dim] = length
        face_low = (node_pos == 0).reshape(shape_b)
        face_high = (node_pos == 7).reshape(shape_b)
        values = values + jnp.where(face_low, jnp.roll(values, 1, which_dim), 0.0) + jnp.where(face_high, jnp.roll(values, -1, which_dim), 0.0)
    return values


def reference(component_share_field, scaled_heat_level, local_transport_value, component_spreading_scale, screened_poisson_reactive_term, expansion_contribution_scale, logarithm_arrhenius_constant, arrhenius_energy_scale, kinetic_exponents, reaction_change_matrix):
    derivative, weights = gll_tables()
    deriv_mat = jnp.asarray(derivative, jnp.float32)
    species_all, size_x, size_y, size_z = component_share_field.shape
    species_solved = component_spreading_scale.shape[0]
    mass_weight = mass_weights(size_x, size_y, size_z, weights)
    multiplicity = multiplicities(size_x, size_y, size_z)
    kinetic_exponents_float = kinetic_exponents.astype(jnp.float32)
    change_matrix_float = reaction_change_matrix.astype(jnp.float32)

    def one_block(block_idx, component_creation_rate):
        offset_length = (block_idx * 8).astype(jnp.int32)
        current_section = lax.dynamic_slice_in_dim(component_share_field, offset_length, 8, 1)
        heat_level_section = lax.dynamic_slice_in_dim(scaled_heat_level, offset_length, 8, 0)
        tile_reaction_speeds = reaction_speeds(current_section, heat_level_section, kinetic_exponents_float, change_matrix_float, logarithm_arrhenius_constant, arrhenius_energy_scale)
        return lax.dynamic_update_slice_in_dim(component_creation_rate, tile_reaction_speeds, offset_length, 1)

    component_creation_rate = lax.fori_loop(0, size_x // 8, one_block, jnp.zeros(component_share_field.shape, jnp.float32))
    expansion_source_field = jnp.einsum("r,retj->etj", expansion_contribution_scale, component_creation_rate, precision=lax.Precision.HIGHEST) / scaled_heat_level
    div_field = shared_sum((mass_weight * expansion_source_field)[None])[0] / (mass_weight * multiplicity)
    diff_cols = component_spreading_scale[:, None, None, None]
    helm_cols = screened_poisson_reactive_term[:, None, None, None]
    carried = component_share_field[:species_solved]
    sources = component_creation_rate[:species_solved]
    rhs = shared_sum(mass_weight * (helm_cols * carried + sources - carried * div_field))
    weighted_cond = local_transport_value * mass_weight
    diag_local = diff_cols * diag_stiffness(weighted_cond, deriv_mat) + helm_cols * mass_weight
    inv_diag = 1.0 / shared_sum(diag_local)
    inv_mult = 1.0 / multiplicity

    def local_dots(first_arr, second_arr):
        return jnp.sum(first_arr * second_arr * inv_mult, axis=(1, 2, 3))

    def operate(values):
        return shared_sum(diff_cols * stiffness(values, weighted_cond, deriv_mat) + helm_cols * mass_weight * values)

    solution = jnp.zeros(rhs.shape, jnp.float32)
    residual = rhs
    precond_res = inv_diag * residual
    direction = precond_res
    resid_dot = local_dots(residual, precond_res)
    for iteration in range(ITERS):
        image = operate(direction)
        step_size = (resid_dot / local_dots(direction, image))[:, None, None, None]
        solution = solution + step_size * direction
        residual = residual - step_size * image
        precond_res = inv_diag * residual
        fresh_dot = local_dots(residual, precond_res)
        direction = precond_res + (fresh_dot / resid_dot)[:, None, None, None] * direction
        resid_dot = fresh_dot
    return solution, div_field
```

```python
import functools

import jax
import jax.numpy as jnp
import numpy as np
from jax import lax
from jax.experimental import pallas as pl
from jax.experimental.pallas import tpu as pltpu
from jax.sharding import PartitionSpec as P

MESH = pl.DeviceIdType.MESH
F32 = jnp.float32
BF16 = jnp.bfloat16
NZ = 12
XY = 64
NS = 16
DIRS = ((-1, 0), (1, 0), (0, -1), (0, 1), (-1, -1), (-1, 1), (1, -1), (1, 1))
OPPOSITE = (1, 0, 3, 2, 7, 6, 5, 4)
SPOTS = (
    [p for p in range(8)],
    [56 + p for p in range(8)],
    [8 * p for p in range(8)],
    [8 * p + 7 for p in range(8)],
    [0],
    [7],
    [56],
    [63],
)


def legendre_seven(points):
    return (429.0 * points**7 - 693.0 * points**5 + 315.0 * points**3 - 35.0 * points) / 16.0


def gll_tables():
    gll_nodes = np.array(
        [
            -1.0,
            -0.8717401485096066,
            -0.5917001814331423,
            -0.2092992179024789,
            0.2092992179024789,
            0.5917001814331423,
            0.8717401485096066,
            1.0,
        ]
    )
    at_nodes = legendre_seven(gll_nodes)
    weights = 2.0 / (56.0 * at_nodes * at_nodes)
    derivative = np.zeros((8, 8))
    for row_index in range(8):
        for col_index in range(8):
            if row_index != col_index:
                derivative[row_index, col_index] = at_nodes[row_index] / (
                    at_nodes[col_index] * (gll_nodes[row_index] - gll_nodes[col_index])
                )
    derivative[0, 0] = -14.0
    derivative[7, 7] = 14.0
    return (derivative, weights)


def constant_table():
    derivative, weights = gll_tables()
    d32 = derivative.astype(np.float32)
    w32 = weights.astype(np.float32)
    square = d32 * d32
    eye8 = np.eye(8, dtype=np.float32)
    eye16 = np.eye(16, dtype=np.float32)
    along_z = np.kron(eye16, d32)
    plane = np.kron(square.T, eye8) + np.kron(eye8, square.T)
    mass = (w32[:, None, None] * w32[None, :, None]) * np.tile(w32, 16)[None, None, :]
    ends = np.array([2.0, 1, 1, 1, 1, 1, 1, 2.0], np.float32)
    mult = (ends[:, None, None] * ends[None, :, None]) * np.tile(ends, 16)[None, None, :]
    return np.concatenate(
        [
            along_z.T,
            along_z,
            np.kron(eye16, square),
            np.pad(plane, ((0, 0), (0, 64))),
            mass.reshape(64, 128),
            mult.reshape(64, 128),
        ],
        0,
    ).astype(np.float32)


def half_matrices(matrix):
    flipped = matrix[:4, ::-1][:, :4]
    even = 0.5 * (matrix[:4, :4] + flipped)
    odd = 0.5 * (matrix[:4, :4] - flipped)
    return [[float(np.float32(v)) for v in row] for row in even], [
        [float(np.float32(v)) for v in row] for row in odd
    ]


FORWARD = half_matrices(gll_tables()[0])
BACKWARD = half_matrices(gll_tables()[0].T)


def apply_line(values, halves):
    even_mat, odd_mat = halves
    even = [values[j] + values[7 - j] for j in range(4)]
    odd = [values[j] - values[7 - j] for j in range(4)]
    low, high = [], []
    for i in range(4):
        first = even_mat[i][0] * even[0]
        second = odd_mat[i][0] * odd[0]
        for j in range(1, 4):
            first = first + even_mat[i][j] * even[j]
            second = second + odd_mat[i][j] * odd[j]
        low.append(second + first)
        high.append(second - first)
    return low + high[::-1]


def stiff_line(values, weights):
    slopes = apply_line(values, FORWARD)
    return apply_line([s * w for s, w in zip(slopes, weights)], BACKWARD)


def pieces(value):
    first = value.astype(BF16)
    rest = value - first.astype(F32)
    second = rest.astype(BF16)
    third = (rest - second.astype(F32)).astype(BF16)
    return first, second, third


def kernel(nz, ny, ng, *refs):
    ins, outs, rest = refs[:11], refs[11:13], refs[13:]
    loads, rest = rest[:11], rest[11:]
    (
        ee_ref,
        cc_ref,
        g_ref,
        wrow_ref,
        diag_ref,
        div_ref,
        my_ref,
        mp_ref,
        wb_ref,
        hm_ref,
        inv_ref,
        z_ref,
        v_ref,
        y_ref,
        sface,
        scorn,
        rface,
        rcorn,
        srow,
        rrow,
        load_sem,
        send_sem,
        recv_sem,
        row_send,
        row_recv,
    ) = rest
    share, heat, cond, diff1, helm1, expn1, loga1, ea1, kin, chg, table = loads
    out_ref, divout_ref = outs

    gx = lax.axis_index("gx")
    gy = lax.axis_index("gy")
    at_y = lax.div(gx, nz)
    at_z = lax.rem(gx, nz)
    nx = nz * ny

    def neighbour(d):
        sx, sy = DIRS[d]
        return (lax.rem(gx + (sx + nx), nx), lax.rem(gy + (sy + ng), ng))

    def peer_g(k):
        return (gx, lax.rem(gy + k, ng))

    def peer_y(k):
        return (lax.rem(at_y + k, ny) * nz + at_z, gy)

    def peer_z(k):
        return (at_y * nz + lax.rem(at_z + k, nz), gy)

    barrier = pltpu.get_barrier_semaphore()
    greeted = [neighbour(d) for d in range(8)]
    greeted += [peer_g(k) for k in range(1, ng)]
    greeted += [peer_y(k) for k in range(1, ny)]
    greeted += [peer_z(k) for k in range(1, nz)]

    fetch = [pltpu.make_async_copy(ins[i], loads[i], load_sem.at[i]) for i in range(11)]
    for one in fetch:
        one.start()
    for device in greeted:
        pl.semaphore_signal(barrier, inc=1, device_id=device, device_id_type=MESH)
    for one in fetch:
        one.wait()

    lane = lax.broadcasted_iota(jnp.int32, (NS, 128), 1)
    sub = lax.broadcasted_iota(jnp.int32, (NS, 128), 0)
    node = lane & 7
    first_node = node == 0
    last_node = node == 7

    def column(row, rows):
        at_lane = lax.broadcasted_iota(jnp.int32, (rows, row.shape[1]), 1)
        at_sub = lax.broadcasted_iota(jnp.int32, (rows, row.shape[1]), 0)
        spread = jnp.broadcast_to(row, (rows, row.shape[1]))
        return jnp.sum(jnp.where(at_lane == at_sub, spread, 0.0), axis=1, keepdims=True)

    def zsum(value):
        before = pltpu.roll(value, 1, 1)
        after = pltpu.roll(value, 127, 1)
        count = value.shape[0]
        return value + jnp.where(
            first_node[:count], before, jnp.where(last_node[:count], after, 0.0)
        )

    diff = jnp.broadcast_to(column(diff1[...], NS), (NS, 128))
    helm = jnp.broadcast_to(column(helm1[...], NS), (NS, 128))

    ea = column(ea1[...], 128)
    const = column(loga1[...], 128) + ea
    ee_ref[...] = jnp.zeros((128, 128), F32)
    ee_ref[:, 0:32] = kin[...].astype(F32)
    base = ee_ref[...]
    base = base + pltpu.roll(base, 32, 1) + pltpu.roll(base, 64, 1)
    ea_p = [p.astype(F32) for p in pieces(-ea)]
    co_p = [p.astype(F32) for p in pieces(const)]
    lane128 = lax.broadcasted_iota(jnp.int32, (128, 128), 1)
    extra = [ea_p[0], ea_p[0], ea_p[0], ea_p[1], ea_p[1], ea_p[2], co_p[0], co_p[1], co_p[2]]
    for i, col in enumerate(extra):
        base = jnp.where(lane128 == 96 + i, col, base)
    ee_ref[...] = base
    change = chg[...].astype(F32)
    weighted = jnp.sum(column(expn1[...], 32) * change, axis=0, keepdims=True)
    we_p = [p.astype(F32) for p in pieces(weighted)]
    sub16 = lax.broadcasted_iota(jnp.int32, (NS, 128), 0)
    tail = jnp.where(
        sub16 == 0,
        we_p[0],
        jnp.where(sub16 == 1, we_p[1], jnp.where(sub16 == 2, we_p[2], 0.0)),
    )
    cc_ref[0:16, :] = change[:16]
    cc_ref[16:32, :] = tail

    inverse = 1.0 / heat[...]
    in_p = pieces(inverse)
    for i in range(3):
        g_ref[i] = in_p[i].astype(F32)
    g_ref[3] = inverse * table[448:512, :]

    wrow_ref[...] = cond[...] * table[448:512, :]
    diag_ref[...] = jnp.dot(
        table[384:448, 0:64], wrow_ref[...], precision=lax.Precision.HIGHEST, preferred_element_type=F32
    ) + jnp.dot(
        wrow_ref[...], table[256:384, :], precision=lax.Precision.HIGHEST, preferred_element_type=F32
    )

    def spread_rows(at, carry):
        mass = jnp.broadcast_to(table[pl.ds(448 + at, 1), :], (NS, 128))
        wb_ref[at] = jnp.broadcast_to(wrow_ref[pl.ds(at, 1), :], (NS, 128))
        hm_ref[at] = helm * mass
        my_ref[at] = mass * share[pl.ds(at, NS, stride=XY), :]
        return carry

    lax.fori_loop(0, XY, spread_rows, 0)

    def chem(first):
        logs, gparts = [], []
        for j in range(4):
            logs.append(jnp.log(share[pl.ds(first + j, 32, stride=XY), :]))
            rows = [jnp.broadcast_to(g_ref[i, pl.ds(first + j, 1), :], (NS, 128)) for i in range(3)]
            one = jnp.where(
                (sub == 0) | (sub == 3) | (sub == 5),
                rows[0],
                jnp.where((sub == 1) | (sub == 4), rows[1], jnp.where(sub == 2, rows[2], 1.0)),
            )
            gparts.append(one)
        log_p = pieces(jnp.concatenate(logs, axis=1))
        gpart = jnp.concatenate(gparts, axis=1).astype(BF16)
        stacked = jnp.concatenate([*log_p, gpart, gpart], axis=0)
        exponent = jnp.dot(ee_ref[...].astype(BF16), stacked, preferred_element_type=F32)
        prog = jnp.concatenate(pieces(jnp.exp(exponent)), axis=0)
        made = cc_ref[...].astype(BF16)
        made = jnp.dot(jnp.concatenate([made, made, made], axis=1), prog, preferred_element_type=F32)
        for j in range(4):
            at = first + j
            part = made[:, 128 * j : 128 * (j + 1)]
            mp_ref[at] = table[pl.ds(448 + at, 1), :] * part[:NS]
            total = part[16:17] + part[17:18] + part[18:19]
            div_ref[pl.ds(at, 1), :] = total * g_ref[3, pl.ds(at, 1), :]

    def chem_ends(i, carry):
        chem(4 * i + 48 * lax.div(i, 2))
        return carry

    def chem_mid(i, carry):
        chem(8 + 4 * i)
        return carry

    def pack(stage, d, field, scalar):
        spots = SPOTS[d]
        if d < 4:
            for p, at in enumerate(spots):
                sface[stage, d, 16 * p : 16 * p + 16, :] = field[at]
            if scalar is not None:
                sface[stage, d, 128:136, :] = scalar[pl.ds(spots[0], 8, stride=spots[1] - spots[0]), :]
        else:
            at = spots[0]
            scorn[stage, d - 4, 0:16, :] = field[at]
            if scalar is not None:
                scorn[stage, d - 4, 16:24, :] = jnp.broadcast_to(scalar[at : at + 1, :], (8, 128))

    def transfer(stage, d):
        if d < 4:
            source, target = sface.at[stage, d], rface.at[stage, d]
            if stage == 2:
                source, target = source.at[0:128], target.at[0:128]
        else:
            source, target = scorn.at[stage, d - 4], rcorn.at[stage, d - 4]
            if stage == 2:
                source, target = source.at[0:16], target.at[0:16]
        return pltpu.make_async_remote_copy(
            src_ref=source,
            dst_ref=target,
            send_sem=send_sem.at[8 * stage + d],
            recv_sem=recv_sem.at[8 * stage + d],
            device_id=neighbour(d),
            device_id_type=MESH,
        )

    def unpack(stage, d, field, scalar):
        spots = SPOTS[OPPOSITE[d]]
        if d < 4:
            for p, at in enumerate(spots):
                field[at] = field[at] + rface[stage, d, 16 * p : 16 * p + 16, :]
            if scalar is not None:
                where = pl.ds(spots[0], 8, stride=spots[1] - spots[0])
                scalar[where, :] = scalar[where, :] + rface[stage, d, 128:136, :]
        else:
            at = spots[0]
            field[at] = field[at] + rcorn[stage, d - 4, 0:16, :]
            if scalar is not None:
                scalar[at : at + 1, :] = scalar[at : at + 1, :] + rcorn[stage, d - 4, 16:17, :]

    sent = []

    def send(stage, d, field, scalar):
        pack(stage, d, field, scalar)
        copy = transfer(stage, d)
        copy.start()
        sent.append((stage, d, copy))

    def collect(stage, field, scalar):
        for at_stage, d, copy in sent:
            if at_stage == stage:
                copy.wait_recv()
                unpack(stage, d, field, scalar)

    lax.fori_loop(0, 4, chem_ends, 0)
    pl.semaphore_wait(barrier, len(greeted))
    for d in range(8):
        send(0, d, my_ref, diag_ref)
    for d in (0, 1, 4, 5, 6, 7):
        send(1, d, mp_ref, div_ref)
    lax.fori_loop(0, 12, chem_mid, 0)
    for d in (2, 3):
        send(1, d, mp_ref, div_ref)

    collect(0, my_ref, diag_ref)
    for x in range(8):
        diag_ref[8 * x : 8 * x + 8, :] = zsum(diag_ref[8 * x : 8 * x + 8, :])

    def invert(at, carry):
        total = diff * diag_ref[pl.ds(at, 1), :] + hm_ref[at] * table[pl.ds(512 + at, 1), :]
        inv_ref[at] = 1.0 / total
        return carry

    lax.fori_loop(0, XY, invert, 0)

    collect(1, mp_ref, div_ref)
    for x in range(8):
        here = slice(8 * x, 8 * x + 8)
        norm = table[448 + 8 * x : 456 + 8 * x, :] * table[512 + 8 * x : 520 + 8 * x, :]
        field = zsum(div_ref[here, :]) / norm
        div_ref[here, :] = field
        divout_ref[here, :] = field

    none = jnp.zeros((NS, 128), F32)

    def share_of(at):
        return 1.0 / table[pl.ds(512 + at, 1), :]

    def start(at, acc):
        local = mp_ref[at] + (helm - div_ref[pl.ds(at, 1), :]) * my_ref[at]
        resid = zsum(local)
        precond = inv_ref[at] * resid
        z_ref[at] = precond
        return acc + resid * precond * share_of(at)

    dot_a = lax.fori_loop(0, XY, start, none)

    def operate(source):
        def z_part(x, carry):
            here = pl.ds(8 * x, 8)
            value = source[here].reshape(128, 128)
            slope = jnp.dot(
                value, table[0:128, :], precision=lax.Precision.HIGHEST, preferred_element_type=F32
            )
            slope = slope * wb_ref[here].reshape(128, 128)
            back = jnp.dot(
                slope, table[128:256, :], precision=lax.Precision.HIGHEST, preferred_element_type=F32
            )
            y_ref[here] = back.reshape(8, NS, 128)
            return carry

        def x_part(y, carry):
            got = stiff_line([source[8 * x + y] for x in range(8)], [wb_ref[8 * x + y] for x in range(8)])
            for x in range(8):
                y_ref[8 * x + y] = y_ref[8 * x + y] + got[x]
            return carry

        def y_part(x, acc):
            values = [source[8 * x + y] for y in range(8)]
            got = stiff_line(values, [wb_ref[8 * x + y] for y in range(8)])
            for y in range(8):
                at = 8 * x + y
                image = diff * (y_ref[at] + got[y]) + hm_ref[at] * values[y]
                y_ref[at] = image
                acc = acc + values[y] * image
            return acc

        lax.fori_loop(0, 8, z_part, 0)
        lax.fori_loop(0, 8, x_part, 0)
        return lax.fori_loop(0, 8, y_part, none)

    dot_c = operate(z_ref)
    for d in range(8):
        send(2, d, y_ref, None)
    collect(2, y_ref, None)

    def second(at, acc):
        image = zsum(y_ref[at])
        precond = inv_ref[at] * image
        v_ref[at] = precond
        return acc + image * precond * share_of(at)

    dot_b = lax.fori_loop(0, XY, second, none)
    dot_d = operate(v_ref)

    packed = none
    for q, acc in enumerate((dot_a, dot_c, dot_b, dot_d)):
        packed = packed + jnp.where(lane == 16 * q + sub, jnp.sum(acc, axis=1, keepdims=True), 0.0)
    row = jnp.sum(packed, axis=0, keepdims=True)

    rows_sent = []
    slot = 0
    for phase, (count, peer) in enumerate(((ng, peer_g), (ny, peer_y), (nz, peer_z))):
        srow[phase] = row
        copies = []
        for k in range(1, count):
            copy = pltpu.make_async_remote_copy(
                src_ref=srow.at[phase],
                dst_ref=rrow.at[slot],
                send_sem=row_send.at[slot],
                recv_sem=row_recv.at[slot],
                device_id=peer(k),
                device_id_type=MESH,
            )
            copy.start()
            copies.append((slot, copy))
            slot += 1
        for _, copy in copies:
            copy.wait_recv()
        for at, _ in copies:
            row = row + rrow[at]
        rows_sent += [copy for _, copy in copies]

    totals = jnp.broadcast_to(row, (NS, 128))
    a, c, b, d = [
        jnp.sum(jnp.where(lane == 16 * q + sub, totals, 0.0), axis=1, keepdims=True) for q in range(4)
    ]
    ratio = b / c
    gamma = (c - ratio * a) / (d - ratio * b)
    alpha = a / c - gamma * ratio
    alpha = jnp.broadcast_to(alpha, (NS, 128))
    gamma = jnp.broadcast_to(gamma, (NS, 128))

    def finish(at, carry):
        out_ref[pl.ds(at, NS, stride=XY), :] = alpha * z_ref[at] + gamma * v_ref[at]
        return carry

    lax.fori_loop(0, XY, finish, 0)

    for _, _, copy in sent:
        copy.wait_send()
    for copy in rows_sent:
        copy.wait_send()


def shards(nz, ny, ng, *args):
    share, heat, cond, diff, helm, expn, loga, ea, kin, chg = args
    count = (ng - 1) + (ny - 1) + (nz - 1)
    operands = [
        share.reshape(32 * XY, 128),
        heat.reshape(XY, 128),
        cond.reshape(XY, 128),
        diff.reshape(1, NS),
        helm.reshape(1, NS),
        expn.reshape(1, 32),
        loga.reshape(1, 128),
        ea.reshape(1, 128),
        kin,
        chg,
        jnp.asarray(constant_table()),
    ]
    cube = pltpu.VMEM((XY, NS, 128), F32)
    out, div = pl.pallas_call(
        functools.partial(kernel, nz, ny, ng),
        out_shape=(
            jax.ShapeDtypeStruct((NS * XY, 128), F32),
            jax.ShapeDtypeStruct((XY, 128), F32),
        ),
        in_specs=[pl.BlockSpec(memory_space=pl.ANY)] * 11,
        out_specs=(
            pl.BlockSpec(memory_space=pltpu.VMEM),
            pl.BlockSpec(memory_space=pltpu.VMEM),
        ),
        scratch_shapes=[pltpu.VMEM(o.shape, o.dtype) for o in operands]
        + [
            pltpu.VMEM((128, 128), F32),
            pltpu.VMEM((32, 128), F32),
            pltpu.VMEM((4, XY, 128), F32),
            pltpu.VMEM((XY, 128), F32),
            pltpu.VMEM((XY, 128), F32),
            pltpu.VMEM((XY, 128), F32),
        ]
        + [cube] * 8
        + [
            pltpu.VMEM((3, 4, 136, 128), F32),
            pltpu.VMEM((3, 4, 24, 128), F32),
            pltpu.VMEM((3, 4, 136, 128), F32),
            pltpu.VMEM((3, 4, 24, 128), F32),
            pltpu.VMEM((3, 1, 128), F32),
            pltpu.VMEM((count, 1, 128), F32),
            pltpu.SemaphoreType.DMA((11,)),
            pltpu.SemaphoreType.DMA((24,)),
            pltpu.SemaphoreType.DMA((24,)),
            pltpu.SemaphoreType.DMA((count,)),
            pltpu.SemaphoreType.DMA((count,)),
        ],
        compiler_params=pltpu.CompilerParams(
            collective_id=0, has_side_effects=True, vmem_limit_bytes=40 * 1024 * 1024
        ),
        name="reacting_step",
    )(*operands)
    return out.reshape(NS, 8, 8, 128), div.reshape(8, 8, 128)


def solution(mesh):
    ng = mesh.shape["gy"]
    ny = mesh.shape["gx"] // NZ
    field = P("gx", "gy", None)
    species = P(None, "gx", "gy", None)
    return jax.shard_map(
        functools.partial(shards, NZ, ny, ng),
        mesh=mesh,
        in_specs=(species, field, field, P(), P(), P(), P(), P(), P(), P()),
        out_specs=(species, field),
        check_vma=False,
    )
```

```python
import functools

import jax
import jax.numpy as jnp
import ml_dtypes
import numpy as np
from jax import lax
from jax.experimental import pallas as pl
from jax.experimental.pallas import tpu as pltpu
from jax.sharding import PartitionSpec as P

MESH = pl.DeviceIdType.MESH
F32 = jnp.float32
BF16 = jnp.bfloat16
NZ = 12
XY = 64
NS = 16
DIRS = ((-1, 0), (1, 0), (0, -1), (0, 1), (-1, -1), (-1, 1), (1, -1), (1, 1))
OPPOSITE = (1, 0, 3, 2, 7, 6, 5, 4)
SPOTS = (
    [p for p in range(8)],
    [56 + p for p in range(8)],
    [8 * p for p in range(8)],
    [8 * p + 7 for p in range(8)],
    [0],
    [7],
    [56],
    [63],
)

EDGES = (
    (1, 0, (1, 0), 6),
    (1, 7, (1, 0), 6),
    (0, 0, (0, 1), 8),
    (7, 0, (0, 1), 8),
)
LOG2E = 1.4426950408889634


def legendre_seven(points):
    return (429.0 * points**7 - 693.0 * points**5 + 315.0 * points**3 - 35.0 * points) / 16.0


def gll_tables():
    gll_nodes = np.array(
        [
            -1.0,
            -0.8717401485096066,
            -0.5917001814331423,
            -0.2092992179024789,
            0.2092992179024789,
            0.5917001814331423,
            0.8717401485096066,
            1.0,
        ]
    )
    at_nodes = legendre_seven(gll_nodes)
    weights = 2.0 / (56.0 * at_nodes * at_nodes)
    derivative = np.zeros((8, 8))
    for row_index in range(8):
        for col_index in range(8):
            if row_index != col_index:
                derivative[row_index, col_index] = at_nodes[row_index] / (
                    at_nodes[col_index] * (gll_nodes[row_index] - gll_nodes[col_index])
                )
    derivative[0, 0] = -14.0
    derivative[7, 7] = 14.0
    return (derivative, weights)


def constant_table():
    derivative, weights = gll_tables()
    d32 = derivative.astype(np.float32)
    w32 = weights.astype(np.float32)
    square = d32 * d32
    eye8 = np.eye(8, dtype=np.float32)
    eye16 = np.eye(16, dtype=np.float32)
    plane = np.kron(square.T, eye8) + np.kron(eye8, square.T)
    mass = (w32[:, None, None] * w32[None, :, None]) * np.tile(w32, 16)[None, None, :]
    ends = np.array([2.0, 1, 1, 1, 1, 1, 1, 2.0], np.float32)
    mult = (ends[:, None, None] * ends[None, :, None]) * np.tile(ends, 16)[None, None, :]
    mass, mult = mass.reshape(64, 128), mult.reshape(64, 128)
    return np.concatenate(
        [mass, mult, 1.0 / mult, np.pad(plane, ((0, 0), (0, 64))), np.kron(eye16, square)], 0
    ).astype(np.float32)


MASS, MULT, SHARE, PLANE, SQUARE = 0, 64, 128, 192, 256


def slope_table():
    along_z = np.kron(np.eye(16, dtype=np.float32), gll_tables()[0].astype(np.float32))
    both = []
    for matrix in (along_z.T, along_z):
        first = matrix.astype(ml_dtypes.bfloat16)
        rest = matrix - first.astype(np.float32)
        second = rest.astype(ml_dtypes.bfloat16)
        third = (rest - second.astype(np.float32)).astype(ml_dtypes.bfloat16)
        both.append(
            np.concatenate(
                [
                    np.concatenate([first, first], 0),
                    np.concatenate([second, second], 0),
                    np.concatenate([third, first], 0),
                ],
                1,
            )
        )
    return np.stack(both)


def half_matrices(matrix):
    flipped = matrix[:4, ::-1][:, :4]
    even = 0.5 * (matrix[:4, :4] + flipped)
    odd = 0.5 * (matrix[:4, :4] - flipped)
    return [[float(np.float32(v)) for v in row] for row in even], [
        [float(np.float32(v)) for v in row] for row in odd
    ]


FORWARD = half_matrices(gll_tables()[0])
BACKWARD = half_matrices(gll_tables()[0].T)


def apply_line(values, halves):
    even_mat, odd_mat = halves
    even = [values[j] + values[7 - j] for j in range(4)]
    odd = [values[j] - values[7 - j] for j in range(4)]
    low, high = [], []
    for i in range(4):
        first = even_mat[i][0] * even[0]
        second = odd_mat[i][0] * odd[0]
        for j in range(1, 4):
            first = first + even_mat[i][j] * even[j]
            second = second + odd_mat[i][j] * odd[j]
        low.append(second + first)
        high.append(second - first)
    return low + high[::-1]


def stiff_line(values, weights):
    slopes = apply_line(values, FORWARD)
    return apply_line([s * w for s, w in zip(slopes, weights)], BACKWARD)


def pieces(value):
    first = value.astype(BF16)
    rest = value - first.astype(F32)
    second = rest.astype(BF16)
    third = (rest - second.astype(F32)).astype(BF16)
    return first, second, third


def kernel(nz, ny, ng, *refs):
    ins, outs, rest = refs[:12], refs[12:14], refs[14:]
    loads, rest = rest[:12], rest[12:]
    (
        ee_ref,
        cc_ref,
        g_ref,
        wrow_ref,
        diag_ref,
        div_ref,
        my_ref,
        mp_ref,
        wb_ref,
        hm_ref,
        inv_ref,
        z_ref,
        v_ref,
        y_ref,
        sface,
        scorn,
        rface,
        rcorn,
        lface,
        lcorn,
        srow,
        rrow,
        load_sem,
        send_sem,
        recv_sem,
        row_send,
        row_recv,
    ) = rest
    share, heat, cond, diff1, helm1, expn1, loga1, ea1, kin, chg, table, slopes = loads
    out_ref, divout_ref = outs

    gx = lax.axis_index("gx")
    gy = lax.axis_index("gy")
    at_y = lax.div(gx, nz)
    at_z = lax.rem(gx, nz)
    nx = nz * ny

    def neighbour(d):
        sx, sy = DIRS[d]
        return (lax.rem(gx + (sx + nx), nx), lax.rem(gy + (sy + ng), ng))

    def peer_g(k):
        return (gx, lax.rem(gy + k, ng))

    def peer_y(k):
        return (lax.rem(at_y + k, ny) * nz + at_z, gy)

    def peer_z(k):
        return (at_y * nz + lax.rem(at_z + k, nz), gy)

    barrier = pltpu.get_barrier_semaphore()
    greeted = [neighbour(d) for d in range(8)]
    greeted += [peer_g(k) for k in range(1, ng)]
    greeted += [peer_y(k) for k in range(1, ny)]
    greeted += [peer_z(k) for k in range(1, nz)]

    fetch = [pltpu.make_async_copy(ins[i], loads[i], load_sem.at[i]) for i in range(12)]
    for one in fetch:
        one.start()
    for device in greeted:
        pl.semaphore_signal(barrier, inc=1, device_id=device, device_id_type=MESH)
    for one in fetch[1:11]:
        one.wait()

    lane = lax.broadcasted_iota(jnp.int32, (NS, 128), 1)
    sub = lax.broadcasted_iota(jnp.int32, (NS, 128), 0)

    def column(row, rows):
        at_lane = lax.broadcasted_iota(jnp.int32, (rows, row.shape[1]), 1)
        at_sub = lax.broadcasted_iota(jnp.int32, (rows, row.shape[1]), 0)
        spread = jnp.broadcast_to(row, (rows, row.shape[1]))
        return jnp.sum(jnp.where(at_lane == at_sub, spread, 0.0), axis=1, keepdims=True)

    def zsum(value):
        before = pltpu.roll(value, 1, 1)
        after = pltpu.roll(value, 127, 1)
        node = lax.broadcasted_iota(jnp.int32, value.shape, 1) & 7
        return value + jnp.where(node == 0, before, jnp.where(node == 7, after, 0.0))

    def rows(ref, first, count):
        return jnp.stack([jnp.broadcast_to(ref[pl.ds(first + i, 1), :], (NS, 128)) for i in range(count)])

    diff = jnp.broadcast_to(column(diff1[...], NS), (NS, 128))
    helm = jnp.broadcast_to(column(helm1[...], NS), (NS, 128))

    scaled = LOG2E * ea1[...]
    ea_p = [p.astype(F32) for p in pieces(-scaled)]
    co_p = [p.astype(F32) for p in pieces(LOG2E * loga1[...] + scaled)]
    sub32 = lax.broadcasted_iota(jnp.int32, (32, 128), 0)
    extra = jnp.zeros((32, 128), F32)
    for i, row in enumerate([ea_p[0], ea_p[0], ea_p[0], ea_p[1], ea_p[1], ea_p[2], *co_p]):
        extra = jnp.where(sub32 == i, row, extra)
    order = kin[...].astype(F32)
    ee_ref[...] = jnp.transpose(jnp.concatenate([order, order, order, extra], axis=0)).astype(BF16)
    change = chg[...].astype(F32)
    weighted = jnp.sum(column(expn1[...], 32) * change, axis=0, keepdims=True)
    we_p = [p.astype(F32) for p in pieces(weighted)]
    tail = jnp.where(
        sub == 0, we_p[0], jnp.where(sub == 1, we_p[1], jnp.where(sub == 2, we_p[2], 0.0))
    )
    made_by = jnp.concatenate([change[:NS], tail], axis=0).astype(BF16)
    cc_ref[:, 0:128] = made_by
    cc_ref[:, 128:256] = made_by

    inverse = 1.0 / heat[...]
    in_p = pieces(inverse)
    for i in range(3):
        g_ref[i] = in_p[i].astype(F32)
    g_ref[3] = inverse * table[MASS : MASS + 64, :]

    wrow_ref[...] = cond[...] * table[MASS : MASS + 64, :]
    diag_ref[...] = jnp.dot(
        table[PLANE : PLANE + 64, 0:64],
        wrow_ref[...],
        precision=lax.Precision.HIGHEST,
        preferred_element_type=F32,
    ) + jnp.dot(
        wrow_ref[...],
        table[SQUARE : SQUARE + 128, :],
        precision=lax.Precision.HIGHEST,
        preferred_element_type=F32,
    )
    fetch[0].wait()

    def chem(first, x, y):
        logs, gparts = [], []
        for j in range(4):
            own = share[pl.ds(first + j, 32, stride=XY), :]
            my_ref[x, y + j] = table[pl.ds(MASS + first + j, 1), :] * own[:NS]
            logs.append(LOG2E * jnp.log(own))
            part = [jnp.broadcast_to(g_ref[i, pl.ds(first + j, 1), :], (NS, 128)) for i in range(3)]
            gparts.append(
                jnp.where(
                    (sub == 0) | (sub == 3) | (sub == 5),
                    part[0],
                    jnp.where((sub == 1) | (sub == 4), part[1], jnp.where(sub == 2, part[2], 1.0)),
                )
            )
        log_p = pieces(jnp.concatenate(logs, axis=1))
        gpart = jnp.concatenate(gparts, axis=1).astype(BF16)
        stacked = jnp.concatenate([*log_p, gpart, gpart], axis=0)
        prog = jnp.exp2(jnp.dot(ee_ref[...], stacked, preferred_element_type=F32))
        high = prog.astype(BF16)
        low = (prog - high.astype(F32)).astype(BF16)
        made = jnp.dot(
            cc_ref[...], jnp.concatenate([high, low], axis=0), preferred_element_type=F32
        )
        for j in range(4):
            at = first + j
            here = made[:, 128 * j : 128 * (j + 1)]
            mp_ref[x, y + j] = table[pl.ds(MASS + at, 1), :] * here[:NS]
            total = here[16:17] + here[17:18] + here[18:19]
            div_ref[pl.ds(at, 1), :] = total * g_ref[3, pl.ds(at, 1), :]

    def chem_plane(x):
        chem(8 * x, x, 0)
        chem(8 * x + 4, x, 4)

    def chem_ends(i, carry):
        chem_plane(7 * i)
        return carry

    def chem_mid(i, carry):
        chem_plane(1 + i)
        return carry

    def pack(stage, d, field, scalar):
        spots = SPOTS[d]
        if d < 4:
            for p, at in enumerate(spots):
                sface[stage, d, 16 * p : 16 * p + 16, :] = field(at)
            sface[stage, d, 128:136, :] = scalar[pl.ds(spots[0], 8, stride=spots[1] - spots[0]), :]
        else:
            at = spots[0]
            scorn[stage, d - 4, 0:16, :] = field(at)
            scorn[stage, d - 4, 16:24, :] = jnp.broadcast_to(scalar[at : at + 1, :], (8, 128))

    started = []

    def launch(stage, d, source, target):
        copy = pltpu.make_async_remote_copy(
            src_ref=source,
            dst_ref=target,
            send_sem=send_sem.at[8 * stage + d],
            recv_sem=recv_sem.at[8 * stage + d],
            device_id=neighbour(d),
            device_id_type=MESH,
        )
        copy.start()
        started.append((stage, d, copy))

    def send(stage, d, field, scalar):
        pack(stage, d, field, scalar)
        if d < 4:
            launch(stage, d, sface.at[stage, d], rface.at[stage, d])
        else:
            launch(stage, d, scorn.at[stage, d - 4], rcorn.at[stage, d - 4])

    def await_from(stage, which):
        for at_stage, d, copy in started:
            if at_stage == stage and d in which:
                copy.wait_recv()

    def add_scalars(stage, scalar):
        for d in range(8):
            spots = SPOTS[OPPOSITE[d]]
            if d < 4:
                where = pl.ds(spots[0], 8, stride=spots[1] - spots[0])
                scalar[where, :] = scalar[where, :] + rface[stage, d, 128:136, :]
            else:
                at = spots[0]
                scalar[at : at + 1, :] = scalar[at : at + 1, :] + rcorn[stage, d - 4, 16:17, :]

    def arrived(stage, x, y):
        parts = []
        for d in range(8):
            spots = SPOTS[OPPOSITE[d]]
            if 8 * x + y not in spots:
                continue
            p = spots.index(8 * x + y)
            if stage == 2:
                parts.append(lface[d, p] if d < 4 else lcorn[d - 4])
            elif d < 4:
                parts.append(rface[stage, d, 16 * p : 16 * p + 16, :])
            else:
                parts.append(rcorn[stage, d - 4, 0:16, :])
        return functools.reduce(lambda a, b: a + b, parts)

    def my_spot(at):
        return table[MASS + at : MASS + at + 1, :] * share[pl.ds(at, NS, stride=XY), :]

    def mp_spot(at):
        return mp_ref[at // 8, at % 8]

    lax.fori_loop(0, 2, chem_ends, 0)
    pl.semaphore_wait(barrier, len(greeted))
    for d in range(8):
        send(0, d, my_spot, diag_ref)
    for d in (0, 1, 4, 5, 6, 7):
        send(1, d, mp_spot, div_ref)
    lax.fori_loop(0, 6, chem_mid, 0)
    for d in (2, 3):
        send(1, d, mp_spot, div_ref)

    none = jnp.zeros((NS, 128), F32)

    await_from(0, range(8))
    add_scalars(0, diag_ref)
    for x in range(8):
        diag_ref[8 * x : 8 * x + 8, :] = zsum(diag_ref[8 * x : 8 * x + 8, :])

    def invert(x, carry):
        wb_ref[x] = rows(wrow_ref, 8 * x, 8)
        hm = helm * rows(table, MASS + 8 * x, 8)
        hm_ref[x] = hm
        inv_ref[x] = 1.0 / (diff * rows(diag_ref, 8 * x, 8) + hm * rows(table, MULT + 8 * x, 8))
        return carry

    lax.fori_loop(0, 8, invert, 0)

    def divergence(x):
        here = slice(8 * x, 8 * x + 8)
        norm = table[MASS + 8 * x : MASS + 8 * x + 8, :] * table[MULT + 8 * x : MULT + 8 * x + 8, :]
        divout_ref[here, :] = zsum(div_ref[here, :]) / norm

    def flat_zsum(value):
        return zsum(value.reshape(-1, 128)).reshape(value.shape)

    def begin(x, y, step, count, made, carried, acc):
        first, jump = 8 * x + y, 8 * step[0] + step[1]
        spots = [(x + i * step[0], y + i * step[1]) for i in range(count)]
        div = jnp.stack(
            [jnp.broadcast_to(divout_ref[pl.ds(first + i * jump, 1), :], (NS, 128)) for i in range(count)]
        )
        part = jnp.stack(
            [
                jnp.broadcast_to(table[pl.ds(SHARE + first + i * jump, 1), :], (NS, 128))
                for i in range(count)
            ]
        )
        resid = flat_zsum(made + (helm - div) * carried)
        inv = jnp.stack([inv_ref[a, b] for a, b in spots])
        precond = inv * resid
        for i, (a, b) in enumerate(spots):
            z_ref[a, b] = precond[i]
        return acc + jnp.sum(resid * precond * part, axis=0)

    def advance(x, y, step, count, image, acc):
        first, jump = 8 * x + y, 8 * step[0] + step[1]
        spots = [(x + i * step[0], y + i * step[1]) for i in range(count)]
        part = jnp.stack(
            [
                jnp.broadcast_to(table[pl.ds(SHARE + first + i * jump, 1), :], (NS, 128))
                for i in range(count)
            ]
        )
        image = flat_zsum(image)
        inv = jnp.stack([inv_ref[a, b] for a, b in spots])
        precond = inv * image
        for i, (a, b) in enumerate(spots):
            v_ref[a, b] = precond[i]
        return acc + jnp.sum(image * precond * part, axis=0)

    def with_edges(field, stage, x, y, step, count):
        spots = [(x + i * step[0], y + i * step[1]) for i in range(count)]
        return jnp.stack([field[a, b] + arrived(stage, a, b) for a, b in spots])

    for x in range(1, 7):
        divergence(x)

    def begin_inside(i, acc):
        x = 1 + i
        return begin(x, 1, (0, 1), 6, mp_ref[x, 1:7], my_ref[x, 1:7], acc)

    dot_a = lax.fori_loop(0, 6, begin_inside, none)
    await_from(1, range(8))
    add_scalars(1, div_ref)
    for x in range(8):
        divergence(x)
    for x, y, step, count in EDGES:
        made = with_edges(mp_ref, 1, x, y, step, count)
        carried = with_edges(my_ref, 0, x, y, step, count)
        dot_a = begin(x, y, step, count, made, carried, dot_a)

    fetch[11].wait()

    def slope_product(value, which):
        first, second, third = pieces(value)
        wide = jnp.dot(
            jnp.concatenate([first, second], axis=1),
            slopes[which, :, 0:256],
            preferred_element_type=F32,
        )
        thin = jnp.dot(
            jnp.concatenate([first, third], axis=1),
            slopes[which, :, 256:384],
            preferred_element_type=F32,
        )
        return wide[:, 0:128] + wide[:, 128:256] + thin

    def yz_part(planes, weights):
        value = jnp.concatenate([p.reshape(128, 128) for p in planes], axis=0)
        weight = jnp.concatenate([w.reshape(128, 128) for w in weights], axis=0)
        back = slope_product(slope_product(value, 0) * weight, 1)
        result = []
        for i, (p, w) in enumerate(zip(planes, weights)):
            lines = jnp.stack(stiff_line([p[y] for y in range(8)], [w[y] for y in range(8)]))
            result.append(back[128 * i : 128 * (i + 1)].reshape(8, NS, 128) + lines)
        return result

    def operate(source, faces_done):
        planes = [source[0], source[7]]
        got = yz_part(planes, [wb_ref[0], wb_ref[7]])
        y_ref[0] = got[0]
        y_ref[7] = got[1]

        def x_part(y, acc):
            values = [source[x, y] for x in range(8)]
            got = stiff_line(values, [wb_ref[x, y] for x in range(8)])
            for x in range(1, 7):
                y_ref[x, y] = got[x]
            for x in (0, 7):
                image = diff * (y_ref[x, y] + got[x]) + hm_ref[x, y] * values[x]
                y_ref[x, y] = image
                acc = acc + values[x] * image
            return acc

        total = lax.fori_loop(0, 8, x_part, none)
        faces_done()

        def rest_part(i, acc):
            first = 1 + 2 * i
            planes = [source[first], source[first + 1]]
            got = yz_part(planes, [wb_ref[first], wb_ref[first + 1]])
            for j in range(2):
                image = diff * (y_ref[first + j] + got[j]) + hm_ref[first + j] * planes[j]
                y_ref[first + j] = image
                acc = acc + jnp.sum(planes[j] * image, axis=0)
            return acc

        return lax.fori_loop(0, 3, rest_part, total)

    def send_faces():
        for d, x in ((0, 0), (1, 7)):
            launch(2, d, y_ref.at[x], lface.at[d])
        for d in range(4, 8):
            at = SPOTS[d][0]
            launch(2, d, y_ref.at[at // 8, at % 8], lcorn.at[d - 4])

    dot_c = operate(z_ref, send_faces)
    for d, y in ((2, 0), (3, 7)):
        launch(2, d, y_ref.at[:, y], lface.at[d])

    def advance_inside(i, acc):
        x = 1 + i
        return advance(x, 1, (0, 1), 6, y_ref[x, 1:7], acc)

    dot_b = lax.fori_loop(0, 6, advance_inside, none)
    await_from(2, range(8))
    for x, y, step, count in EDGES:
        dot_b = advance(x, y, step, count, with_edges(y_ref, 2, x, y, step, count), dot_b)
    for stage, _, copy in started:
        copy.wait_send()
    dot_d = operate(v_ref, lambda: None)

    packed = none
    for q, acc in enumerate((dot_a, dot_c, dot_b, dot_d)):
        packed = packed + jnp.where(lane == 16 * q + sub, jnp.sum(acc, axis=1, keepdims=True), 0.0)
    row = jnp.sum(packed, axis=0, keepdims=True)

    rows_sent = []
    slot = 0
    for phase, (count, peer) in enumerate(((ng, peer_g), (ny, peer_y), (nz, peer_z))):
        srow[phase] = row
        copies = []
        for k in range(1, count):
            copy = pltpu.make_async_remote_copy(
                src_ref=srow.at[phase],
                dst_ref=rrow.at[slot],
                send_sem=row_send.at[slot],
                recv_sem=row_recv.at[slot],
                device_id=peer(k),
                device_id_type=MESH,
            )
            copy.start()
            copies.append((slot, copy))
            slot += 1
        for _, copy in copies:
            copy.wait_recv()
        for at, _ in copies:
            row = row + rrow[at]
        rows_sent += [copy for _, copy in copies]

    totals = jnp.broadcast_to(row, (NS, 128))
    a, c, b, d = [
        jnp.sum(jnp.where(lane == 16 * q + sub, totals, 0.0), axis=1, keepdims=True) for q in range(4)
    ]
    ratio = b / c
    gamma = (c - ratio * a) / (d - ratio * b)
    alpha = a / c - gamma * ratio
    alpha = jnp.broadcast_to(alpha, (NS, 128))
    gamma = jnp.broadcast_to(gamma, (NS, 128))

    def finish(x, carry):
        for y in range(8):
            out_ref[pl.ds(8 * x + y, NS, stride=XY), :] = alpha * z_ref[x, y] + gamma * v_ref[x, y]
        return carry

    lax.fori_loop(0, 8, finish, 0)
    for copy in rows_sent:
        copy.wait_send()


def shards(nz, ny, ng, *args):
    share, heat, cond, diff, helm, expn, loga, ea, kin, chg = args
    count = (ng - 1) + (ny - 1) + (nz - 1)
    operands = [
        share.reshape(32 * XY, 128),
        heat.reshape(XY, 128),
        cond.reshape(XY, 128),
        diff.reshape(1, NS),
        helm.reshape(1, NS),
        expn.reshape(1, 32),
        loga.reshape(1, 128),
        ea.reshape(1, 128),
        kin.T,
        chg,
        jnp.asarray(constant_table()),
        jnp.asarray(slope_table()),
    ]
    cube = pltpu.VMEM((8, 8, NS, 128), F32)
    out, div = pl.pallas_call(
        functools.partial(kernel, nz, ny, ng),
        out_shape=(
            jax.ShapeDtypeStruct((NS * XY, 128), F32),
            jax.ShapeDtypeStruct((XY, 128), F32),
        ),
        in_specs=[pl.BlockSpec(memory_space=pltpu.HBM)] * 12,
        out_specs=(
            pl.BlockSpec(memory_space=pltpu.VMEM),
            pl.BlockSpec(memory_space=pltpu.VMEM),
        ),
        scratch_shapes=[pltpu.VMEM(o.shape, o.dtype) for o in operands]
        + [
            pltpu.VMEM((128, 128), BF16),
            pltpu.VMEM((32, 256), BF16),
            pltpu.VMEM((4, XY, 128), F32),
            pltpu.VMEM((XY, 128), F32),
            pltpu.VMEM((XY, 128), F32),
            pltpu.VMEM((XY, 128), F32),
        ]
        + [cube] * 8
        + [
            pltpu.VMEM((2, 4, 136, 128), F32),
            pltpu.VMEM((2, 4, 24, 128), F32),
            pltpu.VMEM((2, 4, 136, 128), F32),
            pltpu.VMEM((2, 4, 24, 128), F32),
            pltpu.VMEM((4, 8, NS, 128), F32),
            pltpu.VMEM((4, NS, 128), F32),
            pltpu.VMEM((3, 1, 128), F32),
            pltpu.VMEM((count, 1, 128), F32),
            pltpu.SemaphoreType.DMA((12,)),
            pltpu.SemaphoreType.DMA((24,)),
            pltpu.SemaphoreType.DMA((24,)),
            pltpu.SemaphoreType.DMA((count,)),
            pltpu.SemaphoreType.DMA((count,)),
        ],
        compiler_params=pltpu.CompilerParams(
            collective_id=0, has_side_effects=True, vmem_limit_bytes=40 * 1024 * 1024
        ),
        name="reacting_step",
    )(*operands)
    return out.reshape(NS, 8, 8, 128), div.reshape(8, 8, 128)


def solution(mesh):
    ng = mesh.shape["gy"]
    ny = mesh.shape["gx"] // NZ
    field = P("gx", "gy", None)
    species = P(None, "gx", "gy", None)
    return jax.shard_map(
        functools.partial(shards, NZ, ny, ng),
        mesh=mesh,
        in_specs=(species, field, field, P(), P(), P(), P(), P(), P(), P()),
        out_specs=(species, field),
        check_vma=False,
    )
```

```python
import functools

import jax
import jax.numpy as jnp
import ml_dtypes
import numpy as np
from jax import lax
from jax.experimental import pallas as pl
from jax.experimental.pallas import tpu as pltpu
from jax.sharding import PartitionSpec as P

MESH = pl.DeviceIdType.MESH
F32 = jnp.float32
BF16 = jnp.bfloat16
NZ = 12
XY = 64
NS = 16
DIRS = ((-1, 0), (1, 0), (0, -1), (0, 1), (-1, -1), (-1, 1), (1, -1), (1, 1))
OPPOSITE = (1, 0, 3, 2, 7, 6, 5, 4)
SPOTS = (
    [p for p in range(8)],
    [56 + p for p in range(8)],
    [8 * p for p in range(8)],
    [8 * p + 7 for p in range(8)],
    [0],
    [7],
    [56],
    [63],
)

EDGES = (
    (1, 0, (1, 0), 6),
    (1, 7, (1, 0), 6),
    (0, 0, (0, 1), 8),
    (7, 0, (0, 1), 8),
)
LOG2E = 1.4426950408889634


def legendre_seven(points):
    return (429.0 * points**7 - 693.0 * points**5 + 315.0 * points**3 - 35.0 * points) / 16.0


def gll_tables():
    gll_nodes = np.array(
        [
            -1.0,
            -0.8717401485096066,
            -0.5917001814331423,
            -0.2092992179024789,
            0.2092992179024789,
            0.5917001814331423,
            0.8717401485096066,
            1.0,
        ]
    )
    at_nodes = legendre_seven(gll_nodes)
    weights = 2.0 / (56.0 * at_nodes * at_nodes)
    derivative = np.zeros((8, 8))
    for row_index in range(8):
        for col_index in range(8):
            if row_index != col_index:
                derivative[row_index, col_index] = at_nodes[row_index] / (
                    at_nodes[col_index] * (gll_nodes[row_index] - gll_nodes[col_index])
                )
    derivative[0, 0] = -14.0
    derivative[7, 7] = 14.0
    return (derivative, weights)


def constant_table():
    derivative, weights = gll_tables()
    d32 = derivative.astype(np.float32)
    w32 = weights.astype(np.float32)
    square = d32 * d32
    eye8 = np.eye(8, dtype=np.float32)
    eye16 = np.eye(16, dtype=np.float32)
    plane = np.kron(square.T, eye8) + np.kron(eye8, square.T)
    mass = (w32[:, None, None] * w32[None, :, None]) * np.tile(w32, 16)[None, None, :]
    ends = np.array([2.0, 1, 1, 1, 1, 1, 1, 2.0], np.float32)
    mult = (ends[:, None, None] * ends[None, :, None]) * np.tile(ends, 16)[None, None, :]
    mass, mult = mass.reshape(64, 128), mult.reshape(64, 128)
    return np.concatenate(
        [mass, mult, 1.0 / mult, np.pad(plane, ((0, 0), (0, 64))), np.kron(eye16, square)], 0
    ).astype(np.float32)


MASS, MULT, SHARE, PLANE, SQUARE = 0, 64, 128, 192, 256


def slope_table():
    along_z = np.kron(np.eye(16, dtype=np.float32), gll_tables()[0].astype(np.float32))
    both = []
    for matrix in (along_z.T, along_z):
        first = matrix.astype(ml_dtypes.bfloat16)
        rest = matrix - first.astype(np.float32)
        second = rest.astype(ml_dtypes.bfloat16)
        third = (rest - second.astype(np.float32)).astype(ml_dtypes.bfloat16)
        both.append(
            np.concatenate(
                [
                    np.concatenate([first, first], 0),
                    np.concatenate([second, second], 0),
                    np.concatenate([third, first], 0),
                ],
                1,
            )
        )
    return np.stack(both)


def half_matrices(matrix):
    flipped = matrix[:4, ::-1][:, :4]
    even = 0.5 * (matrix[:4, :4] + flipped)
    odd = 0.5 * (matrix[:4, :4] - flipped)
    return [[float(np.float32(v)) for v in row] for row in even], [
        [float(np.float32(v)) for v in row] for row in odd
    ]


FORWARD = half_matrices(gll_tables()[0])
BACKWARD = half_matrices(gll_tables()[0].T)


def apply_line(values, halves):
    even_mat, odd_mat = halves
    even = [values[j] + values[7 - j] for j in range(4)]
    odd = [values[j] - values[7 - j] for j in range(4)]
    low, high = [], []
    for i in range(4):
        first = even_mat[i][0] * even[0]
        second = odd_mat[i][0] * odd[0]
        for j in range(1, 4):
            first = first + even_mat[i][j] * even[j]
            second = second + odd_mat[i][j] * odd[j]
        low.append(second + first)
        high.append(second - first)
    return low + high[::-1]


def stiff_line(values, weights):
    slopes = apply_line(values, FORWARD)
    return apply_line([s * w for s, w in zip(slopes, weights)], BACKWARD)


def pieces(value):
    first = value.astype(BF16)
    rest = value - first.astype(F32)
    second = rest.astype(BF16)
    third = (rest - second.astype(F32)).astype(BF16)
    return first, second, third


def kernel(nz, ny, ng, *refs):
    ins, outs, rest = refs[:12], refs[12:17], refs[17:]
    loads, rest = rest[:12], rest[12:]
    (
        ee_ref,
        cc_ref,
        g_ref,
        wrow_ref,
        diag_ref,
        div_ref,
        my_ref,
        mp_ref,
        wb_ref,
        hm_ref,
        inv_ref,
        z_ref,
        v_ref,
        y_ref,
        rface,
        rcorn,
        spair,
        rpair,
        divout_ref,
        zt_ref,
        vt_ref,
        srow,
        rrow,
        load_sem,
        store_sem,
        send_sem,
        recv_sem,
        row_send,
        row_recv,
    ) = rest
    share, heat, cond, diff1, helm1, expn1, loga1, ea1, kin, chg, table, slopes = loads
    zt_out, vt_out, div_out, alpha_ref, gamma_ref = outs

    gx = lax.axis_index("gx")
    gy = lax.axis_index("gy")
    at_y = lax.div(gx, nz)
    at_z = lax.rem(gx, nz)
    nx = nz * ny

    def neighbour(d):
        sx, sy = DIRS[d]
        return (lax.rem(gx + (sx + nx), nx), lax.rem(gy + (sy + ng), ng))

    def peer_g(k):
        return (gx, lax.rem(gy + k, ng))

    def peer_y(k):
        return (lax.rem(at_y + k, ny) * nz + at_z, gy)

    def peer_z(k):
        return (at_y * nz + lax.rem(at_z + k, nz), gy)

    barrier = pltpu.get_barrier_semaphore()
    greeted = [neighbour(d) for d in range(8)]
    greeted += [peer_g(k) for k in range(1, ng)]
    greeted += [peer_y(k) for k in range(1, ny)]
    greeted += [peer_z(k) for k in range(1, nz)]

    fetch = [pltpu.make_async_copy(ins[i], loads[i], load_sem.at[i]) for i in range(12)]
    for one in fetch:
        one.start()
    for device in greeted:
        pl.semaphore_signal(barrier, inc=1, device_id=device, device_id_type=MESH)
    for one in fetch[1:11]:
        one.wait()

    lane = lax.broadcasted_iota(jnp.int32, (NS, 128), 1)
    sub = lax.broadcasted_iota(jnp.int32, (NS, 128), 0)

    def column(row, rows):
        at_lane = lax.broadcasted_iota(jnp.int32, (rows, row.shape[1]), 1)
        at_sub = lax.broadcasted_iota(jnp.int32, (rows, row.shape[1]), 0)
        spread = jnp.broadcast_to(row, (rows, row.shape[1]))
        return jnp.sum(jnp.where(at_lane == at_sub, spread, 0.0), axis=1, keepdims=True)

    def zsum(value):
        before = pltpu.roll(value, 1, 1)
        after = pltpu.roll(value, 127, 1)
        node = lax.broadcasted_iota(jnp.int32, value.shape, 1) & 7
        return value + jnp.where(node == 0, before, jnp.where(node == 7, after, 0.0))

    def rows(ref, first, count):
        return jnp.stack([jnp.broadcast_to(ref[pl.ds(first + i, 1), :], (NS, 128)) for i in range(count)])

    diff = jnp.broadcast_to(column(diff1[...], NS), (NS, 128))
    helm = jnp.broadcast_to(column(helm1[...], NS), (NS, 128))

    scaled = LOG2E * ea1[...]
    ea_p = [p.astype(F32) for p in pieces(-scaled)]
    co_p = [p.astype(F32) for p in pieces(LOG2E * loga1[...] + scaled)]
    sub32 = lax.broadcasted_iota(jnp.int32, (32, 128), 0)
    extra = jnp.zeros((32, 128), F32)
    for i, row in enumerate([ea_p[0], ea_p[0], ea_p[0], ea_p[1], ea_p[1], ea_p[2], *co_p]):
        extra = jnp.where(sub32 == i, row, extra)
    order = kin[...].astype(F32)
    ee_ref[...] = jnp.transpose(jnp.concatenate([order, order, order, extra], axis=0)).astype(BF16)
    change = chg[...].astype(F32)
    weighted = jnp.sum(column(expn1[...], 32) * change, axis=0, keepdims=True)
    we_p = [p.astype(F32) for p in pieces(weighted)]
    tail = jnp.where(
        sub == 0, we_p[0], jnp.where(sub == 1, we_p[1], jnp.where(sub == 2, we_p[2], 0.0))
    )
    made_by = jnp.concatenate([change[:NS], tail], axis=0).astype(BF16)
    cc_ref[:, 0:128] = made_by
    cc_ref[:, 128:256] = made_by

    inverse = 1.0 / heat[...]
    in_p = pieces(inverse)
    for i in range(3):
        g_ref[i] = in_p[i].astype(F32)
    g_ref[3] = inverse * table[MASS : MASS + 64, :]

    wrow_ref[...] = cond[...] * table[MASS : MASS + 64, :]
    diag_ref[...] = jnp.dot(
        table[PLANE : PLANE + 64, 0:64],
        wrow_ref[...],
        precision=lax.Precision.HIGHEST,
        preferred_element_type=F32,
    ) + jnp.dot(
        wrow_ref[...],
        table[SQUARE : SQUARE + 128, :],
        precision=lax.Precision.HIGHEST,
        preferred_element_type=F32,
    )
    fetch[0].wait()

    started = []

    def launch(stage, d, source, target):
        copy = pltpu.make_async_remote_copy(
            src_ref=source,
            dst_ref=target,
            send_sem=send_sem.at[8 * stage + d],
            recv_sem=recv_sem.at[8 * stage + d],
            device_id=neighbour(d),
            device_id_type=MESH,
        )
        copy.start()
        started.append((stage, d, copy))

    def send(stage, d, field):
        x, y = SPOTS[d][0] // 8, SPOTS[d][0] % 8
        if d < 2:
            launch(stage, d, field.at[x], rface.at[stage, d])
        elif d < 4:
            launch(stage, d, field.at[:, y], rface.at[stage, d])
        else:
            launch(stage, d, field.at[x, y], rcorn.at[stage, d - 4])

    def send_scalars(d):
        spots = SPOTS[d]
        for i, scalar in enumerate((diag_ref, div_ref)):
            if d < 4:
                tile = scalar[pl.ds(spots[0], 8, stride=spots[1] - spots[0]), :]
            else:
                tile = jnp.broadcast_to(scalar[spots[0] : spots[0] + 1, :], (8, 128))
            spair[d, 8 * i : 8 * i + 8, :] = tile
        launch(3, d, spair.at[d], rpair.at[d])

    def await_from(stage, which):
        for at_stage, d, copy in started:
            if at_stage == stage and d in which:
                copy.wait_recv()

    def add_scalars():
        for i, scalar in enumerate((diag_ref, div_ref)):
            for d in range(8):
                spots = SPOTS[OPPOSITE[d]]
                if d < 4:
                    where = pl.ds(spots[0], 8, stride=spots[1] - spots[0])
                    scalar[where, :] = scalar[where, :] + rpair[d, 8 * i : 8 * i + 8, :]
                else:
                    at = spots[0]
                    scalar[at : at + 1, :] = scalar[at : at + 1, :] + rpair[d, 8 * i : 8 * i + 1, :]

    def arrived(stage, x, y):
        parts = []
        for d in range(8):
            spots = SPOTS[OPPOSITE[d]]
            if 8 * x + y in spots:
                p = spots.index(8 * x + y)
                parts.append(rface[stage, d, p] if d < 4 else rcorn[stage, d - 4])
        return functools.reduce(lambda a, b: a + b, parts)

    def chem(spots, inside):
        logs, gparts = [], []
        for x, y in spots:
            at = 8 * x + y
            own = share[pl.ds(at, 32, stride=XY), :]
            if inside:
                my_ref[x, y] = table[pl.ds(MASS + at, 1), :] * own[:NS]
            logs.append(LOG2E * jnp.log(own))
            part = [jnp.broadcast_to(g_ref[i, pl.ds(at, 1), :], (NS, 128)) for i in range(3)]
            gparts.append(
                jnp.where(
                    (sub == 0) | (sub == 3) | (sub == 5),
                    part[0],
                    jnp.where((sub == 1) | (sub == 4), part[1], jnp.where(sub == 2, part[2], 1.0)),
                )
            )
        log_p = pieces(jnp.concatenate(logs, axis=1))
        gpart = jnp.concatenate(gparts, axis=1).astype(BF16)
        stacked = jnp.concatenate([*log_p, gpart, gpart], axis=0)
        prog = jnp.exp2(jnp.dot(ee_ref[...], stacked, preferred_element_type=F32))
        high = prog.astype(BF16)
        low = (prog - high.astype(F32)).astype(BF16)
        made = jnp.dot(
            cc_ref[...], jnp.concatenate([high, low], axis=0), preferred_element_type=F32
        )
        for j, (x, y) in enumerate(spots):
            at = 8 * x + y
            here = made[:, 128 * j : 128 * (j + 1)]
            mp_ref[x, y] = table[pl.ds(MASS + at, 1), :] * here[:NS]
            total = here[16:17] + here[17:18] + here[18:19]
            div_ref[pl.ds(at, 1), :] = total * g_ref[3, pl.ds(at, 1), :]

    def chem_sides(i, carry):
        for j in range(2):
            x = 4 * i + 2 * j
            chem([(x, 0), (x, 7), (x + 1, 0), (x + 1, 7)], False)
        return carry

    def chem_inside(i, carry):
        for j in range(2):
            chem([(1 + 2 * i + j, y) for y in range(1, 7)], True)
        return carry

    for x in range(8):
        for y in range(8):
            if x in (0, 7) or y in (0, 7):
                at = 8 * x + y
                my_ref[x, y] = table[MASS + at : MASS + at + 1, :] * share[pl.ds(at, NS, stride=XY), :]
    pl.semaphore_wait(barrier, len(greeted))
    for d in range(8):
        send(0, d, my_ref)
    chem([(0, y) for y in range(1, 7)], False)
    chem([(7, y) for y in range(1, 7)], False)
    lax.fori_loop(0, 2, chem_sides, 0)
    for d in range(8):
        send_scalars(d)
    for d in range(8):
        send(1, d, mp_ref)
    lax.fori_loop(0, 3, chem_inside, 0)

    none = jnp.zeros((NS, 128), F32)

    await_from(3, range(8))
    add_scalars()
    for x in range(8):
        diag_ref[8 * x : 8 * x + 8, :] = zsum(diag_ref[8 * x : 8 * x + 8, :])

    def invert(x, carry):
        wb_ref[x] = rows(wrow_ref, 8 * x, 8)
        hm = helm * rows(table, MASS + 8 * x, 8)
        hm_ref[x] = hm
        inv_ref[x] = 1.0 / (diff * rows(diag_ref, 8 * x, 8) + hm * rows(table, MULT + 8 * x, 8))
        return carry

    lax.fori_loop(0, 8, invert, 0)

    def divergence(x):
        here = slice(8 * x, 8 * x + 8)
        norm = table[MASS + 8 * x : MASS + 8 * x + 8, :] * table[MULT + 8 * x : MULT + 8 * x + 8, :]
        divout_ref[here, :] = zsum(div_ref[here, :]) / norm

    def flat_zsum(value):
        return zsum(value.reshape(-1, 128)).reshape(value.shape)

    def begin(x, y, step, count, made, carried, acc):
        first, jump = 8 * x + y, 8 * step[0] + step[1]
        spots = [(x + i * step[0], y + i * step[1]) for i in range(count)]
        div = jnp.stack(
            [jnp.broadcast_to(divout_ref[pl.ds(first + i * jump, 1), :], (NS, 128)) for i in range(count)]
        )
        part = jnp.stack(
            [
                jnp.broadcast_to(table[pl.ds(SHARE + first + i * jump, 1), :], (NS, 128))
                for i in range(count)
            ]
        )
        resid = flat_zsum(made + (helm - div) * carried)
        inv = jnp.stack([inv_ref[a, b] for a, b in spots])
        precond = inv * resid
        for i, (a, b) in enumerate(spots):
            z_ref[a, b] = precond[i]
        return acc + jnp.sum(resid * precond * part, axis=0)

    def advance(x, y, step, count, image, acc):
        first, jump = 8 * x + y, 8 * step[0] + step[1]
        spots = [(x + i * step[0], y + i * step[1]) for i in range(count)]
        part = jnp.stack(
            [
                jnp.broadcast_to(table[pl.ds(SHARE + first + i * jump, 1), :], (NS, 128))
                for i in range(count)
            ]
        )
        image = flat_zsum(image)
        inv = jnp.stack([inv_ref[a, b] for a, b in spots])
        precond = inv * image
        for i, (a, b) in enumerate(spots):
            v_ref[a, b] = precond[i]
        return acc + jnp.sum(image * precond * part, axis=0)

    def with_edges(field, stage, x, y, step, count):
        spots = [(x + i * step[0], y + i * step[1]) for i in range(count)]
        return jnp.stack([field[a, b] + arrived(stage, a, b) for a, b in spots])

    for x in range(8):
        divergence(x)
    store_div = pltpu.make_async_copy(divout_ref, div_out, store_sem.at[0])
    store_div.start()

    def begin_inside(i, acc):
        x = 1 + i
        return begin(x, 1, (0, 1), 6, mp_ref[x, 1:7], my_ref[x, 1:7], acc)

    dot_a = lax.fori_loop(0, 6, begin_inside, none)
    await_from(0, range(8))
    await_from(1, range(8))
    for x, y, step, count in EDGES:
        made = with_edges(mp_ref, 1, x, y, step, count)
        carried = with_edges(my_ref, 0, x, y, step, count)
        dot_a = begin(x, y, step, count, made, carried, dot_a)

    fetch[11].wait()

    def slope_product(value, which):
        first, second, third = pieces(value)
        wide = jnp.dot(
            jnp.concatenate([first, second], axis=1),
            slopes[which, :, 0:256],
            preferred_element_type=F32,
        )
        thin = jnp.dot(
            jnp.concatenate([first, third], axis=1),
            slopes[which, :, 256:384],
            preferred_element_type=F32,
        )
        return wide[:, 0:128] + wide[:, 128:256] + thin

    def yz_part(planes, weights):
        value = jnp.concatenate([p.reshape(128, 128) for p in planes], axis=0)
        weight = jnp.concatenate([w.reshape(128, 128) for w in weights], axis=0)
        back = slope_product(slope_product(value, 0) * weight, 1)
        result = []
        for i, (p, w) in enumerate(zip(planes, weights)):
            lines = jnp.stack(stiff_line([p[y] for y in range(8)], [w[y] for y in range(8)]))
            result.append(back[128 * i : 128 * (i + 1)].reshape(8, NS, 128) + lines)
        return result

    def operate(source, faces_done):
        planes = [source[0], source[7]]
        got = yz_part(planes, [wb_ref[0], wb_ref[7]])
        y_ref[0] = got[0]
        y_ref[7] = got[1]

        def x_part(y, acc):
            values = [source[x, y] for x in range(8)]
            got = stiff_line(values, [wb_ref[x, y] for x in range(8)])
            for x in range(1, 7):
                y_ref[x, y] = got[x]
            for x in (0, 7):
                image = diff * (y_ref[x, y] + got[x]) + hm_ref[x, y] * values[x]
                y_ref[x, y] = image
                acc = acc + values[x] * image
            return acc

        total = lax.fori_loop(0, 8, x_part, none)
        faces_done()

        def rest_part(i, acc):
            first = 1 + 2 * i
            planes = [source[first], source[first + 1]]
            got = yz_part(planes, [wb_ref[first], wb_ref[first + 1]])
            for j in range(2):
                image = diff * (y_ref[first + j] + got[j]) + hm_ref[first + j] * planes[j]
                y_ref[first + j] = image
                acc = acc + jnp.sum(planes[j] * image, axis=0)
            return acc

        return lax.fori_loop(0, 3, rest_part, total)

    def send_faces():
        for d in (0, 1, 4, 5, 6, 7):
            send(2, d, y_ref)

    dot_c = operate(z_ref, send_faces)
    for d in (2, 3):
        send(2, d, y_ref)

    def advance_inside(i, acc):
        x = 1 + i
        return advance(x, 1, (0, 1), 6, y_ref[x, 1:7], acc)

    dot_b = lax.fori_loop(0, 6, advance_inside, none)
    await_from(2, range(8))
    for x, y, step, count in EDGES:
        dot_b = advance(x, y, step, count, with_edges(y_ref, 2, x, y, step, count), dot_b)

    def square_x(y, acc):
        slopes_x = apply_line([v_ref[x, y] for x in range(8)], FORWARD)
        return acc + sum(wb_ref[x, y] * slopes_x[x] * slopes_x[x] for x in range(8))

    def square_yz(i, accs):
        acc, mass = accs
        first = 2 * i
        value = v_ref[pl.ds(first, 2)].reshape(256, 128)
        slope_z = slope_product(value, 0)
        for j in range(2):
            plane, weight = v_ref[first + j], wb_ref[first + j]
            slope_y = jnp.stack(apply_line([plane[y] for y in range(8)], FORWARD))
            here = slope_z[128 * j : 128 * (j + 1)].reshape(8, NS, 128)
            acc = acc + jnp.sum(weight * (slope_y * slope_y + here * here), axis=0)
            mass = mass + jnp.sum(hm_ref[first + j] * plane * plane, axis=0)
        return acc, mass

    stiff, mass = lax.fori_loop(0, 4, square_yz, (none, none))
    stiff = lax.fori_loop(0, 8, square_x, stiff)
    dot_d = diff * stiff + mass

    packed = none
    for q, acc in enumerate((dot_a, dot_c, dot_b, dot_d)):
        packed = packed + jnp.where(lane == 16 * q + sub, jnp.sum(acc, axis=1, keepdims=True), 0.0)
    row = jnp.sum(packed, axis=0, keepdims=True)

    def reorder(x, carry):
        for y in range(8):
            where = pl.ds(8 * x + y, NS, stride=XY)
            zt_ref[where, :] = z_ref[x, y]
            vt_ref[where, :] = v_ref[x, y]
        return carry

    store_z = pltpu.make_async_copy(zt_ref, zt_out, store_sem.at[1])
    store_v = pltpu.make_async_copy(vt_ref, vt_out, store_sem.at[2])
    rows_sent = []
    slot = 0
    for phase, (count, peer) in enumerate(((ng, peer_g), (ny, peer_y), (nz, peer_z))):
        srow[phase] = row
        copies = []
        for k in range(1, count):
            copy = pltpu.make_async_remote_copy(
                src_ref=srow.at[phase],
                dst_ref=rrow.at[slot],
                send_sem=row_send.at[slot],
                recv_sem=row_recv.at[slot],
                device_id=peer(k),
                device_id_type=MESH,
            )
            copy.start()
            copies.append((slot, copy))
            slot += 1
        if phase == 0:
            lax.fori_loop(0, 8, reorder, 0)
            store_z.start()
            store_v.start()
        for _, copy in copies:
            copy.wait_recv()
        for at, _ in copies:
            row = row + rrow[at]
        rows_sent += [copy for _, copy in copies]

    totals = jnp.broadcast_to(row, (NS, 128))
    a, c, b, d = [
        jnp.sum(jnp.where(lane == 16 * q + sub, totals, 0.0), axis=1, keepdims=True) for q in range(4)
    ]
    ratio = b / c
    gamma = (c - ratio * a) / (d - ratio * b)
    alpha = a / c - gamma * ratio
    alpha_ref[...] = jnp.broadcast_to(alpha, (NS, 128))
    gamma_ref[...] = jnp.broadcast_to(gamma, (NS, 128))

    for _, _, copy in started:
        copy.wait_send()
    for copy in rows_sent:
        copy.wait_send()
    store_div.wait()
    store_z.wait()
    store_v.wait()


def shards(nz, ny, ng, *args):
    share, heat, cond, diff, helm, expn, loga, ea, kin, chg = args
    count = (ng - 1) + (ny - 1) + (nz - 1)
    operands = [
        share.reshape(32 * XY, 128),
        heat.reshape(XY, 128),
        cond.reshape(XY, 128),
        diff.reshape(1, NS),
        helm.reshape(1, NS),
        expn.reshape(1, 32),
        loga.reshape(1, 128),
        ea.reshape(1, 128),
        kin.T,
        chg,
        jnp.asarray(constant_table()),
        jnp.asarray(slope_table()),
    ]
    cube = pltpu.VMEM((8, 8, NS, 128), F32)
    zt, vt, div, alpha, gamma = pl.pallas_call(
        functools.partial(kernel, nz, ny, ng),
        out_shape=(
            jax.ShapeDtypeStruct((NS * XY, 128), F32),
            jax.ShapeDtypeStruct((NS * XY, 128), F32),
            jax.ShapeDtypeStruct((XY, 128), F32),
            jax.ShapeDtypeStruct((NS, 128), F32),
            jax.ShapeDtypeStruct((NS, 128), F32),
        ),
        in_specs=[pl.BlockSpec(memory_space=pltpu.HBM)] * 12,
        out_specs=(
            pl.BlockSpec(memory_space=pltpu.HBM),
            pl.BlockSpec(memory_space=pltpu.HBM),
            pl.BlockSpec(memory_space=pltpu.HBM),
            pl.BlockSpec(memory_space=pltpu.VMEM),
            pl.BlockSpec(memory_space=pltpu.VMEM),
        ),
        scratch_shapes=[pltpu.VMEM(o.shape, o.dtype) for o in operands]
        + [
            pltpu.VMEM((128, 128), BF16),
            pltpu.VMEM((32, 256), BF16),
            pltpu.VMEM((4, XY, 128), F32),
            pltpu.VMEM((XY, 128), F32),
            pltpu.VMEM((XY, 128), F32),
            pltpu.VMEM((XY, 128), F32),
        ]
        + [cube] * 8
        + [
            pltpu.VMEM((3, 4, 8, NS, 128), F32),
            pltpu.VMEM((3, 4, NS, 128), F32),
            pltpu.VMEM((8, NS, 128), F32),
            pltpu.VMEM((8, NS, 128), F32),
            pltpu.VMEM((XY, 128), F32),
            pltpu.VMEM((NS * XY, 128), F32),
            pltpu.VMEM((NS * XY, 128), F32),
            pltpu.VMEM((3, 1, 128), F32),
            pltpu.VMEM((count, 1, 128), F32),
            pltpu.SemaphoreType.DMA((12,)),
            pltpu.SemaphoreType.DMA((3,)),
            pltpu.SemaphoreType.DMA((32,)),
            pltpu.SemaphoreType.DMA((32,)),
            pltpu.SemaphoreType.DMA((count,)),
            pltpu.SemaphoreType.DMA((count,)),
        ],
        compiler_params=pltpu.CompilerParams(
            collective_id=0, has_side_effects=True, vmem_limit_bytes=67043328
        ),
        name="reacting_step",
    )(*operands)
    zt, vt = zt.reshape(NS, 8, 8, 128), vt.reshape(NS, 8, 8, 128)
    out = alpha[:, None, None, :] * zt + gamma[:, None, None, :] * vt
    return out, div.reshape(8, 8, 128)


def solution(mesh):
    ng = mesh.shape["gy"]
    ny = mesh.shape["gx"] // NZ
    field = P("gx", "gy", None)
    species = P(None, "gx", "gy", None)
    return jax.shard_map(
        functools.partial(shards, NZ, ny, ng),
        mesh=mesh,
        in_specs=(species, field, field, P(), P(), P(), P(), P(), P(), P()),
        out_specs=(species, field),
        check_vma=False,
    )
```

```python
import functools

import jax
import jax.numpy as jnp
import ml_dtypes
import numpy as np
from jax import lax
from jax.experimental import pallas as pl
from jax.experimental.pallas import tpu as pltpu
from jax.sharding import PartitionSpec as P

MESH = pl.DeviceIdType.MESH
F32 = jnp.float32
BF16 = jnp.bfloat16
NZ = 12
XY = 64
NS = 16
DIRS = ((-1, 0), (1, 0), (0, -1), (0, 1), (-1, -1), (-1, 1), (1, -1), (1, 1))
OPPOSITE = (1, 0, 3, 2, 7, 6, 5, 4)
SPOTS = (
    [p for p in range(8)],
    [56 + p for p in range(8)],
    [8 * p for p in range(8)],
    [8 * p + 7 for p in range(8)],
    [0],
    [7],
    [56],
    [63],
)

EDGES = (
    (1, 0, (1, 0), 6),
    (1, 7, (1, 0), 6),
    (0, 0, (0, 1), 8),
    (7, 0, (0, 1), 8),
)
LOG2E = 1.4426950408889634


def legendre_seven(points):
    return (429.0 * points**7 - 693.0 * points**5 + 315.0 * points**3 - 35.0 * points) / 16.0


def gll_tables():
    gll_nodes = np.array(
        [
            -1.0,
            -0.8717401485096066,
            -0.5917001814331423,
            -0.2092992179024789,
            0.2092992179024789,
            0.5917001814331423,
            0.8717401485096066,
            1.0,
        ]
    )
    at_nodes = legendre_seven(gll_nodes)
    weights = 2.0 / (56.0 * at_nodes * at_nodes)
    derivative = np.zeros((8, 8))
    for row_index in range(8):
        for col_index in range(8):
            if row_index != col_index:
                derivative[row_index, col_index] = at_nodes[row_index] / (
                    at_nodes[col_index] * (gll_nodes[row_index] - gll_nodes[col_index])
                )
    derivative[0, 0] = -14.0
    derivative[7, 7] = 14.0
    return (derivative, weights)


def constant_table():
    derivative, weights = gll_tables()
    d32 = derivative.astype(np.float32)
    w32 = weights.astype(np.float32)
    square = d32 * d32
    eye8 = np.eye(8, dtype=np.float32)
    eye16 = np.eye(16, dtype=np.float32)
    plane = np.kron(square.T, eye8) + np.kron(eye8, square.T)
    mass = (w32[:, None, None] * w32[None, :, None]) * np.tile(w32, 16)[None, None, :]
    ends = np.array([2.0, 1, 1, 1, 1, 1, 1, 2.0], np.float32)
    mult = (ends[:, None, None] * ends[None, :, None]) * np.tile(ends, 16)[None, None, :]
    mass, mult = mass.reshape(64, 128), mult.reshape(64, 128)
    return np.concatenate(
        [mass, mult, 1.0 / mult, np.pad(plane, ((0, 0), (0, 64))), np.kron(eye16, square)], 0
    ).astype(np.float32)


MASS, MULT, SHARE, PLANE, SQUARE = 0, 64, 128, 192, 256


def slope_table():
    along_z = np.kron(np.eye(16, dtype=np.float32), gll_tables()[0].astype(np.float32))
    both = []
    for matrix in (along_z.T, along_z):
        first = matrix.astype(ml_dtypes.bfloat16)
        rest = matrix - first.astype(np.float32)
        second = rest.astype(ml_dtypes.bfloat16)
        third = (rest - second.astype(np.float32)).astype(ml_dtypes.bfloat16)
        both.append(
            np.concatenate(
                [
                    np.concatenate([first, first], 0),
                    np.concatenate([second, second], 0),
                    np.concatenate([third, first], 0),
                ],
                1,
            )
        )
    return np.stack(both)


def half_matrices(matrix):
    flipped = matrix[:4, ::-1][:, :4]
    even = 0.5 * (matrix[:4, :4] + flipped)
    odd = 0.5 * (matrix[:4, :4] - flipped)
    return [[float(np.float32(v)) for v in row] for row in even], [
        [float(np.float32(v)) for v in row] for row in odd
    ]


FORWARD = half_matrices(gll_tables()[0])
BACKWARD = half_matrices(gll_tables()[0].T)


def apply_line(values, halves):
    even_mat, odd_mat = halves
    even = [values[j] + values[7 - j] for j in range(4)]
    odd = [values[j] - values[7 - j] for j in range(4)]
    low, high = [], []
    for i in range(4):
        first = even_mat[i][0] * even[0]
        second = odd_mat[i][0] * odd[0]
        for j in range(1, 4):
            first = first + even_mat[i][j] * even[j]
            second = second + odd_mat[i][j] * odd[j]
        low.append(second + first)
        high.append(second - first)
    return low + high[::-1]


def stiff_line(values, weights):
    slopes = apply_line(values, FORWARD)
    return apply_line([s * w for s, w in zip(slopes, weights)], BACKWARD)


def pieces(value):
    first = value.astype(BF16)
    rest = value - first.astype(F32)
    second = rest.astype(BF16)
    third = (rest - second.astype(F32)).astype(BF16)
    return first, second, third


def kernel(nz, ny, ng, *refs):
    ins, outs, rest = refs[:12], refs[12:17], refs[17:]
    loads, rest = rest[:12], rest[12:]
    (
        ee_ref,
        cc_ref,
        g_ref,
        wrow_ref,
        diag_ref,
        div_ref,
        my_ref,
        mp_ref,
        wb_ref,
        hm_ref,
        inv_ref,
        z_ref,
        v_ref,
        y_ref,
        rface,
        rcorn,
        spair,
        rpair,
        divout_ref,
        zt_ref,
        vt_ref,
        srow,
        rrow,
        load_sem,
        store_sem,
        send_sem,
        recv_sem,
        row_send,
        row_recv,
    ) = rest
    share, heat, cond, diff1, helm1, expn1, loga1, ea1, kin, chg, table, slopes = loads
    zt_out, vt_out, div_out, alpha_ref, gamma_ref = outs

    gx = lax.axis_index("gx")
    gy = lax.axis_index("gy")
    at_y = lax.div(gx, nz)
    at_z = lax.rem(gx, nz)
    nx = nz * ny

    def neighbour(d):
        sx, sy = DIRS[d]
        return (lax.rem(gx + (sx + nx), nx), lax.rem(gy + (sy + ng), ng))

    def peer_g(k):
        return (gx, lax.rem(gy + k, ng))

    def peer_y(k):
        return (lax.rem(at_y + k, ny) * nz + at_z, gy)

    def peer_z(k):
        return (at_y * nz + lax.rem(at_z + k, nz), gy)

    barrier = pltpu.get_barrier_semaphore()
    greeted = [neighbour(d) for d in range(8)]
    greeted += [peer_g(k) for k in range(1, ng)]
    greeted += [peer_y(k) for k in range(1, ny)]
    greeted += [peer_z(k) for k in range(1, nz)]

    fetch = [pltpu.make_async_copy(ins[i], loads[i], load_sem.at[i]) for i in range(12)]
    for one in fetch:
        one.start()
    for device in greeted:
        pl.semaphore_signal(barrier, inc=1, device_id=device, device_id_type=MESH)
    for one in fetch[1:11]:
        one.wait()

    lane = lax.broadcasted_iota(jnp.int32, (NS, 128), 1)
    sub = lax.broadcasted_iota(jnp.int32, (NS, 128), 0)

    def column(row, rows):
        at_lane = lax.broadcasted_iota(jnp.int32, (rows, row.shape[1]), 1)
        at_sub = lax.broadcasted_iota(jnp.int32, (rows, row.shape[1]), 0)
        spread = jnp.broadcast_to(row, (rows, row.shape[1]))
        return jnp.sum(jnp.where(at_lane == at_sub, spread, 0.0), axis=1, keepdims=True)

    def zsum(value):
        before = pltpu.roll(value, 1, 1)
        after = pltpu.roll(value, 127, 1)
        node = lax.broadcasted_iota(jnp.int32, value.shape, 1) & 7
        return value + jnp.where(node == 0, before, jnp.where(node == 7, after, 0.0))

    def rows(ref, first, count):
        return jnp.stack([jnp.broadcast_to(ref[pl.ds(first + i, 1), :], (NS, 128)) for i in range(count)])

    diff = jnp.broadcast_to(column(diff1[...], NS), (NS, 128))
    helm = jnp.broadcast_to(column(helm1[...], NS), (NS, 128))

    scaled = LOG2E * ea1[...]
    ea_p = [p.astype(F32) for p in pieces(-scaled)]
    co_p = [p.astype(F32) for p in pieces(LOG2E * loga1[...] + scaled)]
    sub32 = lax.broadcasted_iota(jnp.int32, (32, 128), 0)
    extra = jnp.zeros((32, 128), F32)
    for i, row in enumerate([ea_p[0], ea_p[0], ea_p[0], ea_p[1], ea_p[1], ea_p[2], *co_p]):
        extra = jnp.where(sub32 == i, row, extra)
    order = kin[...].astype(F32)
    ee_ref[...] = jnp.transpose(jnp.concatenate([order, order, order, extra], axis=0)).astype(BF16)
    change = chg[...].astype(F32)
    weighted = jnp.sum(column(expn1[...], 32) * change, axis=0, keepdims=True)
    we_p = [p.astype(F32) for p in pieces(weighted)]
    tail = jnp.where(
        sub == 0, we_p[0], jnp.where(sub == 1, we_p[1], jnp.where(sub == 2, we_p[2], 0.0))
    )
    made_by = jnp.concatenate([change[:NS], tail], axis=0).astype(BF16)
    cc_ref[:, 0:128] = made_by
    cc_ref[:, 128:256] = made_by

    inverse = 1.0 / heat[...]
    in_p = pieces(inverse)
    for i in range(3):
        g_ref[i] = in_p[i].astype(F32)
    g_ref[3] = inverse * table[MASS : MASS + 64, :]

    wrow_ref[...] = cond[...] * table[MASS : MASS + 64, :]
    diag_ref[...] = jnp.dot(
        table[PLANE : PLANE + 64, 0:64],
        wrow_ref[...],
        precision=lax.Precision.HIGHEST,
        preferred_element_type=F32,
    ) + jnp.dot(
        wrow_ref[...],
        table[SQUARE : SQUARE + 128, :],
        precision=lax.Precision.HIGHEST,
        preferred_element_type=F32,
    )
    fetch[0].wait()

    started = []

    def launch(stage, d, source, target):
        copy = pltpu.make_async_remote_copy(
            src_ref=source,
            dst_ref=target,
            send_sem=send_sem.at[8 * stage + d],
            recv_sem=recv_sem.at[8 * stage + d],
            device_id=neighbour(d),
            device_id_type=MESH,
        )
        copy.start()
        started.append((stage, d, copy))

    def send(stage, d, field):
        x, y = SPOTS[d][0] // 8, SPOTS[d][0] % 8
        if d < 2:
            launch(stage, d, field.at[x], rface.at[stage, d])
        elif d < 4:
            launch(stage, d, field.at[:, y], rface.at[stage, d])
        else:
            launch(stage, d, field.at[x, y], rcorn.at[stage, d - 4])

    def send_scalars(d):
        spots = SPOTS[d]
        for i, scalar in enumerate((diag_ref, div_ref)):
            if d < 4:
                tile = scalar[pl.ds(spots[0], 8, stride=spots[1] - spots[0]), :]
            else:
                tile = jnp.broadcast_to(scalar[spots[0] : spots[0] + 1, :], (8, 128))
            spair[d, 8 * i : 8 * i + 8, :] = tile
        launch(3, d, spair.at[d], rpair.at[d])

    def await_from(stage, which):
        for at_stage, d, copy in started:
            if at_stage == stage and d in which:
                copy.wait_recv()

    def add_scalars():
        for i, scalar in enumerate((diag_ref, div_ref)):
            for d in range(8):
                spots = SPOTS[OPPOSITE[d]]
                if d < 4:
                    where = pl.ds(spots[0], 8, stride=spots[1] - spots[0])
                    scalar[where, :] = scalar[where, :] + rpair[d, 8 * i : 8 * i + 8, :]
                else:
                    at = spots[0]
                    scalar[at : at + 1, :] = scalar[at : at + 1, :] + rpair[d, 8 * i : 8 * i + 1, :]

    def arrived(stage, x, y):
        parts = []
        for d in range(8):
            spots = SPOTS[OPPOSITE[d]]
            if 8 * x + y in spots:
                p = spots.index(8 * x + y)
                parts.append(rface[stage, d, p] if d < 4 else rcorn[stage, d - 4])
        return functools.reduce(lambda a, b: a + b, parts)

    def chem(spots, inside):
        logs, gparts = [], []
        for x, y in spots:
            at = 8 * x + y
            own = share[pl.ds(at, 32, stride=XY), :]
            if inside:
                my_ref[x, y] = table[pl.ds(MASS + at, 1), :] * own[:NS]
            logs.append(LOG2E * jnp.log(own))
            part = [jnp.broadcast_to(g_ref[i, pl.ds(at, 1), :], (NS, 128)) for i in range(3)]
            gparts.append(
                jnp.where(
                    (sub == 0) | (sub == 3) | (sub == 5),
                    part[0],
                    jnp.where((sub == 1) | (sub == 4), part[1], jnp.where(sub == 2, part[2], 1.0)),
                )
            )
        log_p = pieces(jnp.concatenate(logs, axis=1))
        gpart = jnp.concatenate(gparts, axis=1).astype(BF16)
        stacked = jnp.concatenate([*log_p, gpart, gpart], axis=0)
        prog = jnp.exp2(jnp.dot(ee_ref[...], stacked, preferred_element_type=F32))
        high = prog.astype(BF16)
        low = (prog - high.astype(F32)).astype(BF16)
        made = jnp.dot(
            cc_ref[...], jnp.concatenate([high, low], axis=0), preferred_element_type=F32
        )
        for j, (x, y) in enumerate(spots):
            at = 8 * x + y
            here = made[:, 128 * j : 128 * (j + 1)]
            mp_ref[x, y] = table[pl.ds(MASS + at, 1), :] * here[:NS]
            total = here[16:17] + here[17:18] + here[18:19]
            div_ref[pl.ds(at, 1), :] = total * g_ref[3, pl.ds(at, 1), :]

    def chem_inside(i, carry):
        for j in range(2):
            chem([(1 + 2 * i + j, y) for y in range(1, 7)], True)
        return carry

    for x in range(8):
        for y in range(8):
            if x in (0, 7) or y in (0, 7):
                at = 8 * x + y
                my_ref[x, y] = table[MASS + at : MASS + at + 1, :] * share[pl.ds(at, NS, stride=XY), :]
    pl.semaphore_wait(barrier, len(greeted))
    for d in range(8):
        send(0, d, my_ref)
    def chem_ends(i, carry):
        chem([(7 * i, y) for y in range(4)], False)
        chem([(7 * i, y) for y in range(4, 8)], False)
        return carry

    def chem_sides(i, carry):
        chem([(1 + i, 0), (1 + i, 7), (4 + i, 0), (4 + i, 7)], False)
        return carry

    lax.fori_loop(0, 2, chem_ends, 0)
    for d in (4, 5, 6, 7, 0, 1):
        send_scalars(d)
        send(1, d, mp_ref)
    lax.fori_loop(0, 3, chem_sides, 0)
    for d in (2, 3):
        send_scalars(d)
        send(1, d, mp_ref)
    lax.fori_loop(0, 3, chem_inside, 0)

    none = jnp.zeros((NS, 128), F32)

    await_from(3, range(8))
    add_scalars()
    for x in range(8):
        diag_ref[8 * x : 8 * x + 8, :] = zsum(diag_ref[8 * x : 8 * x + 8, :])

    def invert(x, carry):
        wb_ref[x] = rows(wrow_ref, 8 * x, 8)
        hm = helm * rows(table, MASS + 8 * x, 8)
        hm_ref[x] = hm
        inv_ref[x] = 1.0 / (diff * rows(diag_ref, 8 * x, 8) + hm * rows(table, MULT + 8 * x, 8))
        return carry

    lax.fori_loop(0, 8, invert, 0)

    def divergence(x):
        here = slice(8 * x, 8 * x + 8)
        norm = table[MASS + 8 * x : MASS + 8 * x + 8, :] * table[MULT + 8 * x : MULT + 8 * x + 8, :]
        divout_ref[here, :] = zsum(div_ref[here, :]) / norm

    def flat_zsum(value):
        return zsum(value.reshape(-1, 128)).reshape(value.shape)

    fetch[11].wait()

    def slope_product(value, which):
        first, second, third = pieces(value)
        wide = jnp.dot(
            jnp.concatenate([first, second], axis=1),
            slopes[which, :, 0:256],
            preferred_element_type=F32,
        )
        thin = jnp.dot(
            jnp.concatenate([first, third], axis=1),
            slopes[which, :, 256:384],
            preferred_element_type=F32,
        )
        return wide[:, 0:128] + wide[:, 128:256] + thin

    def begin(x, y, step, count, made, carried, acc):
        first, jump = 8 * x + y, 8 * step[0] + step[1]
        spots = [(x + i * step[0], y + i * step[1]) for i in range(count)]
        div = jnp.stack(
            [jnp.broadcast_to(divout_ref[pl.ds(first + i * jump, 1), :], (NS, 128)) for i in range(count)]
        )
        part = jnp.stack(
            [
                jnp.broadcast_to(table[pl.ds(SHARE + first + i * jump, 1), :], (NS, 128))
                for i in range(count)
            ]
        )
        resid = flat_zsum(made + (helm - div) * carried)
        inv = jnp.stack([inv_ref[a, b] for a, b in spots])
        precond = inv * resid
        for i, (a, b) in enumerate(spots):
            z_ref[a, b] = precond[i]
        return acc + jnp.sum(resid * precond * part, axis=0), precond

    def advance(x, y, step, count, image, acc):
        first, jump = 8 * x + y, 8 * step[0] + step[1]
        spots = [(x + i * step[0], y + i * step[1]) for i in range(count)]
        part = jnp.stack(
            [
                jnp.broadcast_to(table[pl.ds(SHARE + first + i * jump, 1), :], (NS, 128))
                for i in range(count)
            ]
        )
        image = flat_zsum(image)
        inv = jnp.stack([inv_ref[a, b] for a, b in spots])
        precond = inv * image
        for i, (a, b) in enumerate(spots):
            v_ref[a, b] = precond[i]
        return acc + jnp.sum(image * precond * part, axis=0), precond

    def with_edges(field, stage, x, y, step, count):
        spots = [(x + i * step[0], y + i * step[1]) for i in range(count)]
        return jnp.stack([field[a, b] + arrived(stage, a, b) for a, b in spots])

    for x in range(8):
        divergence(x)
    store_div = pltpu.make_async_copy(divout_ref, div_out, store_sem.at[0])
    store_div.start()

    def z_stiff(values, weights):
        flat = values.reshape(-1, 128)
        back = slope_product(slope_product(flat, 0) * weights.reshape(-1, 128), 1)
        return back.reshape(values.shape)

    def begin_inside(i, acc):
        planes = []
        for j in range(2):
            x = 1 + 2 * i + j
            acc, precond = begin(x, 1, (0, 1), 6, mp_ref[x, 1:7], my_ref[x, 1:7], acc)
            planes.append(precond)
        first = 1 + 2 * i
        weights = jnp.concatenate([wb_ref[first, 1:7], wb_ref[first + 1, 1:7]], axis=0)
        back = z_stiff(jnp.concatenate(planes, axis=0), weights)
        y_ref[first, 1:7] = back[0:6]
        y_ref[first + 1, 1:7] = back[6:12]
        return acc

    def edge_spots():
        return [(x + i * step[0], y + i * step[1]) for x, y, step, count in EDGES for i in range(count)]

    dot_a = lax.fori_loop(0, 3, begin_inside, none)
    await_from(0, range(8))
    await_from(1, range(8))
    values = []
    for x, y, step, count in EDGES:
        made = with_edges(mp_ref, 1, x, y, step, count)
        carried = with_edges(my_ref, 0, x, y, step, count)
        dot_a, precond = begin(x, y, step, count, made, carried, dot_a)
        values.append(precond)
    weights = jnp.stack([wb_ref[x, y] for x, y in edge_spots()])
    back = z_stiff(jnp.concatenate(values, axis=0), weights)
    for i, (x, y) in enumerate(edge_spots()):
        y_ref[x, y] = back[i]

    def y_lines(plane, weight):
        return jnp.stack(stiff_line([plane[y] for y in range(8)], [weight[y] for y in range(8)]))

    def operate(source, faces_done):
        for x in (0, 7):
            y_ref[x] = y_ref[x] + y_lines(source[x], wb_ref[x])

        def x_part(y, acc):
            values = [source[x, y] for x in range(8)]
            got = stiff_line(values, [wb_ref[x, y] for x in range(8)])
            for x in range(1, 7):
                y_ref[x, y] = y_ref[x, y] + got[x]
            for x in (0, 7):
                image = diff * (y_ref[x, y] + got[x]) + hm_ref[x, y] * values[x]
                y_ref[x, y] = image
                acc = acc + values[x] * image
            return acc

        total = lax.fori_loop(0, 8, x_part, none)
        faces_done()

        def rest_part(i, acc):
            for j in range(2):
                x = 1 + 2 * i + j
                plane = source[x]
                image = diff * (y_ref[x] + y_lines(plane, wb_ref[x])) + hm_ref[x] * plane
                y_ref[x] = image
                acc = acc + jnp.sum(plane * image, axis=0)
            return acc

        return lax.fori_loop(0, 3, rest_part, total)

    def send_faces():
        for d in (0, 1, 4, 5, 6, 7):
            send(2, d, y_ref)

    dot_c = operate(z_ref, send_faces)
    for d in (2, 3):
        send(2, d, y_ref)

    def z_square(values, weights):
        slope = slope_product(values.reshape(-1, 128), 0).reshape(values.shape)
        return jnp.sum(weights * slope * slope, axis=0)

    def advance_inside(i, accs):
        acc, stiff = accs
        planes = []
        for j in range(2):
            x = 1 + 2 * i + j
            acc, precond = advance(x, 1, (0, 1), 6, y_ref[x, 1:7], acc)
            planes.append(precond)
        first = 1 + 2 * i
        weights = jnp.concatenate([wb_ref[first, 1:7], wb_ref[first + 1, 1:7]], axis=0)
        return acc, stiff + z_square(jnp.concatenate(planes, axis=0), weights)

    dot_b, stiff = lax.fori_loop(0, 3, advance_inside, (none, none))
    await_from(2, range(8))
    values = []
    for x, y, step, count in EDGES:
        dot_b, precond = advance(x, y, step, count, with_edges(y_ref, 2, x, y, step, count), dot_b)
        values.append(precond)
    weights = jnp.stack([wb_ref[x, y] for x, y in edge_spots()])
    stiff = stiff + z_square(jnp.concatenate(values, axis=0), weights)

    def square_x(y, acc):
        slopes_x = apply_line([v_ref[x, y] for x in range(8)], FORWARD)
        return acc + sum(wb_ref[x, y] * slopes_x[x] * slopes_x[x] for x in range(8))

    def square_y(i, accs):
        acc, mass = accs
        for j in range(2):
            plane, weight = v_ref[2 * i + j], wb_ref[2 * i + j]
            slope_y = jnp.stack(apply_line([plane[y] for y in range(8)], FORWARD))
            acc = acc + jnp.sum(weight * slope_y * slope_y, axis=0)
            mass = mass + jnp.sum(hm_ref[2 * i + j] * plane * plane, axis=0)
        return acc, mass

    stiff, mass = lax.fori_loop(0, 4, square_y, (stiff, none))
    stiff = lax.fori_loop(0, 8, square_x, stiff)
    dot_d = diff * stiff + mass

    packed = none
    for q, acc in enumerate((dot_a, dot_c, dot_b, dot_d)):
        packed = packed + jnp.where(lane == 16 * q + sub, jnp.sum(acc, axis=1, keepdims=True), 0.0)
    row = jnp.sum(packed, axis=0, keepdims=True)

    def reorder(x, carry):
        for y in range(8):
            where = pl.ds(8 * x + y, NS, stride=XY)
            zt_ref[where, :] = z_ref[x, y]
            vt_ref[where, :] = v_ref[x, y]
        return carry

    store_z = pltpu.make_async_copy(zt_ref, zt_out, store_sem.at[1])
    store_v = pltpu.make_async_copy(vt_ref, vt_out, store_sem.at[2])
    rows_sent = []
    slot = 0
    for phase, (count, peer) in enumerate(((ng, peer_g), (ny, peer_y), (nz, peer_z))):
        srow[phase] = row
        copies = []
        for k in range(1, count):
            copy = pltpu.make_async_remote_copy(
                src_ref=srow.at[phase],
                dst_ref=rrow.at[slot],
                send_sem=row_send.at[slot],
                recv_sem=row_recv.at[slot],
                device_id=peer(k),
                device_id_type=MESH,
            )
            copy.start()
            copies.append((slot, copy))
            slot += 1
        if phase == 0:
            lax.fori_loop(0, 8, reorder, 0)
            store_z.start()
            store_v.start()
        for _, copy in copies:
            copy.wait_recv()
        for at, _ in copies:
            row = row + rrow[at]
        rows_sent += [copy for _, copy in copies]

    totals = jnp.broadcast_to(row, (NS, 128))
    a, c, b, d = [
        jnp.sum(jnp.where(lane == 16 * q + sub, totals, 0.0), axis=1, keepdims=True) for q in range(4)
    ]
    ratio = b / c
    gamma = (c - ratio * a) / (d - ratio * b)
    alpha = a / c - gamma * ratio
    alpha_ref[...] = jnp.broadcast_to(alpha, (NS, 128))
    gamma_ref[...] = jnp.broadcast_to(gamma, (NS, 128))

    for _, _, copy in started:
        copy.wait_send()
    for copy in rows_sent:
        copy.wait_send()
    store_div.wait()
    store_z.wait()
    store_v.wait()


def combine(zt, vt, alpha, gamma, div, out, div_out, *scratch):
    z_ref, v_ref, o_ref, a_ref, g_ref, d_ref, in_sem, out_sem = scratch
    small = [
        pltpu.make_async_copy(alpha, a_ref, in_sem.at[8]),
        pltpu.make_async_copy(gamma, g_ref, in_sem.at[9]),
        pltpu.make_async_copy(div, d_ref, in_sem.at[10]),
    ]
    for one in small:
        one.start()
    parts = [slice(256 * i, 256 * i + 256) for i in range(4)]
    come = []
    for i, part in enumerate(parts):
        come.append(
            (
                pltpu.make_async_copy(zt.at[part], z_ref.at[part], in_sem.at[2 * i]),
                pltpu.make_async_copy(vt.at[part], v_ref.at[part], in_sem.at[2 * i + 1]),
            )
        )
        for one in come[i]:
            one.start()
    for one in small:
        one.wait()
    leave = [pltpu.make_async_copy(d_ref, div_out, out_sem.at[4])]
    leave[0].start()
    for i, part in enumerate(parts):
        for one in come[i]:
            one.wait()
        for j in range(4):
            s = 4 * i + j
            here = slice(XY * s, XY * s + XY)
            o_ref[here, :] = a_ref[s : s + 1, :] * z_ref[here, :] + g_ref[s : s + 1, :] * v_ref[here, :]
        leave.append(pltpu.make_async_copy(o_ref.at[part], out.at[part], out_sem.at[i]))
        leave[-1].start()
    for one in leave:
        one.wait()


def shards(nz, ny, ng, *args):
    share, heat, cond, diff, helm, expn, loga, ea, kin, chg = args
    count = (ng - 1) + (ny - 1) + (nz - 1)
    operands = [
        share.reshape(32 * XY, 128),
        heat.reshape(XY, 128),
        cond.reshape(XY, 128),
        diff.reshape(1, NS),
        helm.reshape(1, NS),
        expn.reshape(1, 32),
        loga.reshape(1, 128),
        ea.reshape(1, 128),
        kin.T,
        chg,
        jnp.asarray(constant_table()),
        jnp.asarray(slope_table()),
    ]
    cube = pltpu.VMEM((8, 8, NS, 128), F32)
    zt, vt, div, alpha, gamma = pl.pallas_call(
        functools.partial(kernel, nz, ny, ng),
        out_shape=(
            jax.ShapeDtypeStruct((NS * XY, 128), F32),
            jax.ShapeDtypeStruct((NS * XY, 128), F32),
            jax.ShapeDtypeStruct((XY, 128), F32),
            jax.ShapeDtypeStruct((NS, 128), F32),
            jax.ShapeDtypeStruct((NS, 128), F32),
        ),
        in_specs=[pl.BlockSpec(memory_space=pltpu.HBM)] * 12,
        out_specs=(
            pl.BlockSpec(memory_space=pltpu.HBM),
            pl.BlockSpec(memory_space=pltpu.HBM),
            pl.BlockSpec(memory_space=pltpu.HBM),
            pl.BlockSpec(memory_space=pltpu.VMEM),
            pl.BlockSpec(memory_space=pltpu.VMEM),
        ),
        scratch_shapes=[pltpu.VMEM(o.shape, o.dtype) for o in operands]
        + [
            pltpu.VMEM((128, 128), BF16),
            pltpu.VMEM((32, 256), BF16),
            pltpu.VMEM((4, XY, 128), F32),
            pltpu.VMEM((XY, 128), F32),
            pltpu.VMEM((XY, 128), F32),
            pltpu.VMEM((XY, 128), F32),
        ]
        + [cube] * 8
        + [
            pltpu.VMEM((3, 4, 8, NS, 128), F32),
            pltpu.VMEM((3, 4, NS, 128), F32),
            pltpu.VMEM((8, NS, 128), F32),
            pltpu.VMEM((8, NS, 128), F32),
            pltpu.VMEM((XY, 128), F32),
            pltpu.VMEM((NS * XY, 128), F32),
            pltpu.VMEM((NS * XY, 128), F32),
            pltpu.VMEM((3, 1, 128), F32),
            pltpu.VMEM((count, 1, 128), F32),
            pltpu.SemaphoreType.DMA((12,)),
            pltpu.SemaphoreType.DMA((3,)),
            pltpu.SemaphoreType.DMA((32,)),
            pltpu.SemaphoreType.DMA((32,)),
            pltpu.SemaphoreType.DMA((count,)),
            pltpu.SemaphoreType.DMA((count,)),
        ],
        compiler_params=pltpu.CompilerParams(
            collective_id=0, has_side_effects=True, vmem_limit_bytes=67043328
        ),
        name="reacting_step",
    )(*operands)
    whole = pltpu.VMEM((NS * XY, 128), F32)
    out, div = pl.pallas_call(
        combine,
        out_shape=(
            jax.ShapeDtypeStruct((NS * XY, 128), F32),
            jax.ShapeDtypeStruct((XY, 128), F32),
        ),
        in_specs=[pl.BlockSpec(memory_space=pltpu.HBM)] * 5,
        out_specs=(
            pl.BlockSpec(memory_space=pltpu.HBM),
            pl.BlockSpec(memory_space=pltpu.HBM),
        ),
        scratch_shapes=[
            whole,
            whole,
            whole,
            pltpu.VMEM((NS, 128), F32),
            pltpu.VMEM((NS, 128), F32),
            pltpu.VMEM((XY, 128), F32),
            pltpu.SemaphoreType.DMA((11,)),
            pltpu.SemaphoreType.DMA((5,)),
        ],
        compiler_params=pltpu.CompilerParams(vmem_limit_bytes=67043328),
        name="combine",
    )(zt, vt, alpha, gamma, div)
    return out.reshape(NS, 8, 8, 128), div.reshape(8, 8, 128)


def solution(mesh):
    ng = mesh.shape["gy"]
    ny = mesh.shape["gx"] // NZ
    field = P("gx", "gy", None)
    species = P(None, "gx", "gy", None)
    return jax.shard_map(
        functools.partial(shards, NZ, ny, ng),
        mesh=mesh,
        in_specs=(species, field, field, P(), P(), P(), P(), P(), P(), P()),
        out_specs=(species, field),
        check_vma=False,
    )
```

```python
import functools

import jax
import jax.numpy as jnp
import ml_dtypes
import numpy as np
from jax import lax
from jax.experimental import pallas as pl
from jax.experimental.pallas import tpu as pltpu
from jax.sharding import PartitionSpec as P

MESH = pl.DeviceIdType.MESH
F32 = jnp.float32
BF16 = jnp.bfloat16
NZ = 12
XY = 64
NS = 16
DIRS = ((-1, 0), (1, 0), (0, -1), (0, 1), (-1, -1), (-1, 1), (1, -1), (1, 1))
OPPOSITE = (1, 0, 3, 2, 7, 6, 5, 4)
SPOTS = (
    [p for p in range(8)],
    [56 + p for p in range(8)],
    [8 * p for p in range(8)],
    [8 * p + 7 for p in range(8)],
    [0],
    [7],
    [56],
    [63],
)

EDGES = (
    (1, 0, (1, 0), 6),
    (1, 7, (1, 0), 6),
    (0, 0, (0, 1), 8),
    (7, 0, (0, 1), 8),
)
LOG2E = 1.4426950408889634


def legendre_seven(points):
    return (429.0 * points**7 - 693.0 * points**5 + 315.0 * points**3 - 35.0 * points) / 16.0


def gll_tables():
    gll_nodes = np.array(
        [
            -1.0,
            -0.8717401485096066,
            -0.5917001814331423,
            -0.2092992179024789,
            0.2092992179024789,
            0.5917001814331423,
            0.8717401485096066,
            1.0,
        ]
    )
    at_nodes = legendre_seven(gll_nodes)
    weights = 2.0 / (56.0 * at_nodes * at_nodes)
    derivative = np.zeros((8, 8))
    for row_index in range(8):
        for col_index in range(8):
            if row_index != col_index:
                derivative[row_index, col_index] = at_nodes[row_index] / (
                    at_nodes[col_index] * (gll_nodes[row_index] - gll_nodes[col_index])
                )
    derivative[0, 0] = -14.0
    derivative[7, 7] = 14.0
    return (derivative, weights)


def constant_table():
    derivative, weights = gll_tables()
    d32 = derivative.astype(np.float32)
    w32 = weights.astype(np.float32)
    square = d32 * d32
    eye8 = np.eye(8, dtype=np.float32)
    eye16 = np.eye(16, dtype=np.float32)
    plane = np.kron(square.T, eye8) + np.kron(eye8, square.T)
    mass = (w32[:, None, None] * w32[None, :, None]) * np.tile(w32, 16)[None, None, :]
    ends = np.array([2.0, 1, 1, 1, 1, 1, 1, 2.0], np.float32)
    mult = (ends[:, None, None] * ends[None, :, None]) * np.tile(ends, 16)[None, None, :]
    mass, mult = mass.reshape(64, 128), mult.reshape(64, 128)
    return np.concatenate(
        [mass, mult, 1.0 / mult, np.pad(plane, ((0, 0), (0, 64))), np.kron(eye16, square)], 0
    ).astype(np.float32)


MASS, MULT, SHARE, PLANE, SQUARE = 0, 64, 128, 192, 256


def slope_table():
    along_z = np.kron(np.eye(16, dtype=np.float32), gll_tables()[0].astype(np.float32))
    both = []
    for matrix in (along_z.T, along_z):
        first = matrix.astype(ml_dtypes.bfloat16)
        rest = matrix - first.astype(np.float32)
        second = rest.astype(ml_dtypes.bfloat16)
        third = (rest - second.astype(np.float32)).astype(ml_dtypes.bfloat16)
        both.append(
            np.concatenate(
                [
                    np.concatenate([first, first], 0),
                    np.concatenate([second, second], 0),
                    np.concatenate([third, first], 0),
                ],
                1,
            )
        )
    return np.stack(both)


def half_matrices(matrix):
    flipped = matrix[:4, ::-1][:, :4]
    even = 0.5 * (matrix[:4, :4] + flipped)
    odd = 0.5 * (matrix[:4, :4] - flipped)
    return [[float(np.float32(v)) for v in row] for row in even], [
        [float(np.float32(v)) for v in row] for row in odd
    ]


FORWARD = half_matrices(gll_tables()[0])
BACKWARD = half_matrices(gll_tables()[0].T)


def apply_line(values, halves):
    even_mat, odd_mat = halves
    even = [values[j] + values[7 - j] for j in range(4)]
    odd = [values[j] - values[7 - j] for j in range(4)]
    low, high = [], []
    for i in range(4):
        first = even_mat[i][0] * even[0]
        second = odd_mat[i][0] * odd[0]
        for j in range(1, 4):
            first = first + even_mat[i][j] * even[j]
            second = second + odd_mat[i][j] * odd[j]
        low.append(second + first)
        high.append(second - first)
    return low + high[::-1]


def stiff_line(values, weights):
    slopes = apply_line(values, FORWARD)
    return apply_line([s * w for s, w in zip(slopes, weights)], BACKWARD)


def pieces(value):
    first = value.astype(BF16)
    rest = value - first.astype(F32)
    second = rest.astype(BF16)
    third = (rest - second.astype(F32)).astype(BF16)
    return first, second, third


def kernel(nz, ny, ng, *refs):
    ins, outs, rest = refs[:12], refs[12:17], refs[17:]
    loads, rest = rest[:12], rest[12:]
    (
        ee_ref,
        cc_ref,
        g_ref,
        wrow_ref,
        diag_ref,
        div_ref,
        my_ref,
        mp_ref,
        wb_ref,
        hm_ref,
        inv_ref,
        z_ref,
        v_ref,
        y_ref,
        rface,
        rcorn,
        spair,
        rpair,
        divout_ref,
        zt_ref,
        vt_ref,
        srow,
        rrow,
        load_sem,
        store_sem,
        send_sem,
        recv_sem,
        row_send,
        row_recv,
    ) = rest
    share, heat, cond, diff1, helm1, expn1, loga1, ea1, kin, chg, table, slopes = loads
    zt_out, vt_out, div_out, alpha_ref, gamma_ref = outs

    gx = lax.axis_index("gx")
    gy = lax.axis_index("gy")
    at_y = lax.div(gx, nz)
    at_z = lax.rem(gx, nz)
    nx = nz * ny

    def neighbour(d):
        sx, sy = DIRS[d]
        return (lax.rem(gx + (sx + nx), nx), lax.rem(gy + (sy + ng), ng))

    def peer_g(k):
        return (gx, lax.rem(gy + k, ng))

    def peer_y(k):
        return (lax.rem(at_y + k, ny) * nz + at_z, gy)

    def peer_z(k):
        return (at_y * nz + lax.rem(at_z + k, nz), gy)

    barrier = pltpu.get_barrier_semaphore()
    greeted = [neighbour(d) for d in range(8)]
    greeted += [peer_g(k) for k in range(1, ng)]
    greeted += [peer_y(k) for k in range(1, ny)]
    greeted += [peer_z(k) for k in range(1, nz)]

    fetch = [pltpu.make_async_copy(ins[i], loads[i], load_sem.at[i]) for i in range(12)]
    for one in fetch:
        one.start()
    for device in greeted:
        pl.semaphore_signal(barrier, inc=1, device_id=device, device_id_type=MESH)
    for one in fetch[1:11]:
        one.wait()

    lane = lax.broadcasted_iota(jnp.int32, (NS, 128), 1)
    sub = lax.broadcasted_iota(jnp.int32, (NS, 128), 0)

    def column(row, rows):
        at_lane = lax.broadcasted_iota(jnp.int32, (rows, row.shape[1]), 1)
        at_sub = lax.broadcasted_iota(jnp.int32, (rows, row.shape[1]), 0)
        spread = jnp.broadcast_to(row, (rows, row.shape[1]))
        return jnp.sum(jnp.where(at_lane == at_sub, spread, 0.0), axis=1, keepdims=True)

    def zsum(value):
        before = pltpu.roll(value, 1, 1)
        after = pltpu.roll(value, 127, 1)
        node = lax.broadcasted_iota(jnp.int32, value.shape, 1) & 7
        return value + jnp.where(node == 0, before, jnp.where(node == 7, after, 0.0))

    def rows(ref, first, count):
        return jnp.stack([jnp.broadcast_to(ref[pl.ds(first + i, 1), :], (NS, 128)) for i in range(count)])

    diff = jnp.broadcast_to(column(diff1[...], NS), (NS, 128))
    helm = jnp.broadcast_to(column(helm1[...], NS), (NS, 128))

    scaled = LOG2E * ea1[...]
    ea_p = [p.astype(F32) for p in pieces(-scaled)]
    co_p = [p.astype(F32) for p in pieces(LOG2E * loga1[...] + scaled)]
    sub32 = lax.broadcasted_iota(jnp.int32, (32, 128), 0)
    extra = jnp.zeros((32, 128), F32)
    for i, row in enumerate([ea_p[0], ea_p[0], ea_p[0], ea_p[1], ea_p[1], ea_p[2], *co_p]):
        extra = jnp.where(sub32 == i, row, extra)
    order = kin[...].astype(F32)
    ee_ref[...] = jnp.transpose(jnp.concatenate([order, order, order, extra], axis=0)).astype(BF16)
    change = chg[...].astype(F32)
    weighted = jnp.sum(column(expn1[...], 32) * change, axis=0, keepdims=True)
    we_p = [p.astype(F32) for p in pieces(weighted)]
    tail = jnp.where(
        sub == 0, we_p[0], jnp.where(sub == 1, we_p[1], jnp.where(sub == 2, we_p[2], 0.0))
    )
    made_by = jnp.concatenate([change[:NS], tail], axis=0).astype(BF16)
    cc_ref[:, 0:128] = made_by
    cc_ref[:, 128:256] = made_by

    inverse = 1.0 / heat[...]
    in_p = pieces(inverse)
    for i in range(3):
        g_ref[i] = in_p[i].astype(F32)
    g_ref[3] = inverse * table[MASS : MASS + 64, :]

    wrow_ref[...] = cond[...] * table[MASS : MASS + 64, :]
    diag_ref[...] = jnp.dot(
        table[PLANE : PLANE + 64, 0:64],
        wrow_ref[...],
        precision=lax.Precision.HIGHEST,
        preferred_element_type=F32,
    ) + jnp.dot(
        wrow_ref[...],
        table[SQUARE : SQUARE + 128, :],
        precision=lax.Precision.HIGHEST,
        preferred_element_type=F32,
    )
    fetch[0].wait()

    started = []

    def launch(stage, d, source, target):
        copy = pltpu.make_async_remote_copy(
            src_ref=source,
            dst_ref=target,
            send_sem=send_sem.at[8 * stage + d],
            recv_sem=recv_sem.at[8 * stage + d],
            device_id=neighbour(d),
            device_id_type=MESH,
        )
        copy.start()
        started.append((stage, d, copy))

    def send(stage, d, field):
        x, y = SPOTS[d][0] // 8, SPOTS[d][0] % 8
        if d < 2:
            launch(stage, d, field.at[x], rface.at[stage, d])
        elif d < 4:
            launch(stage, d, field.at[:, y], rface.at[stage, d])
        else:
            launch(stage, d, field.at[x, y], rcorn.at[stage, d - 4])

    def send_scalars(d):
        spots = SPOTS[d]
        for i, scalar in enumerate((diag_ref, div_ref)):
            if d < 4:
                tile = scalar[pl.ds(spots[0], 8, stride=spots[1] - spots[0]), :]
            else:
                tile = jnp.broadcast_to(scalar[spots[0] : spots[0] + 1, :], (8, 128))
            spair[d, 8 * i : 8 * i + 8, :] = tile
        launch(3, d, spair.at[d], rpair.at[d])

    def await_from(stage, which):
        for at_stage, d, copy in started:
            if at_stage == stage and d in which:
                copy.wait_recv()

    def add_scalars():
        for i, scalar in enumerate((diag_ref, div_ref)):
            for d in range(8):
                spots = SPOTS[OPPOSITE[d]]
                if d < 4:
                    where = pl.ds(spots[0], 8, stride=spots[1] - spots[0])
                    scalar[where, :] = scalar[where, :] + rpair[d, 8 * i : 8 * i + 8, :]
                else:
                    at = spots[0]
                    scalar[at : at + 1, :] = scalar[at : at + 1, :] + rpair[d, 8 * i : 8 * i + 1, :]

    def arrived(stage, x, y):
        parts = []
        for d in range(8):
            spots = SPOTS[OPPOSITE[d]]
            if 8 * x + y in spots:
                p = spots.index(8 * x + y)
                parts.append(rface[stage, d, p] if d < 4 else rcorn[stage, d - 4])
        return functools.reduce(lambda a, b: a + b, parts)

    def chem(spots, inside):
        logs, gparts = [], []
        for x, y in spots:
            at = 8 * x + y
            own = share[pl.ds(at, 32, stride=XY), :]
            if inside:
                my_ref[x, y] = table[pl.ds(MASS + at, 1), :] * own[:NS]
            logs.append(LOG2E * jnp.log(own))
            part = [jnp.broadcast_to(g_ref[i, pl.ds(at, 1), :], (NS, 128)) for i in range(3)]
            gparts.append(
                jnp.where(
                    (sub == 0) | (sub == 3) | (sub == 5),
                    part[0],
                    jnp.where((sub == 1) | (sub == 4), part[1], jnp.where(sub == 2, part[2], 1.0)),
                )
            )
        log_p = pieces(jnp.concatenate(logs, axis=1))
        gpart = jnp.concatenate(gparts, axis=1).astype(BF16)
        stacked = jnp.concatenate([*log_p, gpart, gpart], axis=0)
        prog = jnp.exp2(jnp.dot(ee_ref[...], stacked, preferred_element_type=F32))
        high = prog.astype(BF16)
        low = (prog - high.astype(F32)).astype(BF16)
        made = jnp.dot(
            cc_ref[...], jnp.concatenate([high, low], axis=0), preferred_element_type=F32
        )
        for j, (x, y) in enumerate(spots):
            at = 8 * x + y
            here = made[:, 128 * j : 128 * (j + 1)]
            mp_ref[x, y] = table[pl.ds(MASS + at, 1), :] * here[:NS]
            total = here[16:17] + here[17:18] + here[18:19]
            div_ref[pl.ds(at, 1), :] = total * g_ref[3, pl.ds(at, 1), :]

    def chem_inside(i, carry):
        for j in range(2):
            chem([(1 + 2 * i + j, y) for y in range(1, 7)], True)
        return carry

    for x in range(8):
        for y in range(8):
            if x in (0, 7) or y in (0, 7):
                at = 8 * x + y
                my_ref[x, y] = table[MASS + at : MASS + at + 1, :] * share[pl.ds(at, NS, stride=XY), :]
    pl.semaphore_wait(barrier, len(greeted))
    for d in range(8):
        send(0, d, my_ref)
    def chem_ends(i, carry):
        chem([(7 * i, y) for y in range(4)], False)
        chem([(7 * i, y) for y in range(4, 8)], False)
        return carry

    def chem_sides(i, carry):
        chem([(1 + i, 0), (1 + i, 7), (4 + i, 0), (4 + i, 7)], False)
        return carry

    lax.fori_loop(0, 2, chem_ends, 0)
    for d in (4, 5, 6, 7, 0, 1):
        send_scalars(d)
        send(1, d, mp_ref)
    lax.fori_loop(0, 3, chem_sides, 0)
    for d in (2, 3):
        send_scalars(d)
        send(1, d, mp_ref)
    lax.fori_loop(0, 3, chem_inside, 0)

    none = jnp.zeros((NS, 128), F32)

    await_from(3, range(8))
    add_scalars()
    for x in range(8):
        diag_ref[8 * x : 8 * x + 8, :] = zsum(diag_ref[8 * x : 8 * x + 8, :])

    def invert(x, carry):
        wb_ref[x] = rows(wrow_ref, 8 * x, 8)
        hm = helm * rows(table, MASS + 8 * x, 8)
        hm_ref[x] = hm
        inv_ref[x] = 1.0 / (diff * rows(diag_ref, 8 * x, 8) + hm * rows(table, MULT + 8 * x, 8))
        return carry

    lax.fori_loop(0, 8, invert, 0)

    def divergence(x):
        here = slice(8 * x, 8 * x + 8)
        norm = table[MASS + 8 * x : MASS + 8 * x + 8, :] * table[MULT + 8 * x : MULT + 8 * x + 8, :]
        divout_ref[here, :] = zsum(div_ref[here, :]) / norm

    def flat_zsum(value):
        return zsum(value.reshape(-1, 128)).reshape(value.shape)

    fetch[11].wait()

    def slope_product(value, which):
        first, second, third = pieces(value)
        wide = jnp.dot(
            jnp.concatenate([first, second], axis=1),
            slopes[which, :, 0:256],
            preferred_element_type=F32,
        )
        thin = jnp.dot(
            jnp.concatenate([first, third], axis=1),
            slopes[which, :, 256:384],
            preferred_element_type=F32,
        )
        return wide[:, 0:128] + wide[:, 128:256] + thin

    def begin(x, y, step, count, made, carried, acc):
        first, jump = 8 * x + y, 8 * step[0] + step[1]
        spots = [(x + i * step[0], y + i * step[1]) for i in range(count)]
        div = jnp.stack(
            [jnp.broadcast_to(divout_ref[pl.ds(first + i * jump, 1), :], (NS, 128)) for i in range(count)]
        )
        part = jnp.stack(
            [
                jnp.broadcast_to(table[pl.ds(SHARE + first + i * jump, 1), :], (NS, 128))
                for i in range(count)
            ]
        )
        resid = flat_zsum(made + (helm - div) * carried)
        inv = jnp.stack([inv_ref[a, b] for a, b in spots])
        precond = inv * resid
        for i, (a, b) in enumerate(spots):
            z_ref[a, b] = precond[i]
        return acc + jnp.sum(resid * precond * part, axis=0), precond

    def advance(x, y, step, count, image, acc):
        first, jump = 8 * x + y, 8 * step[0] + step[1]
        spots = [(x + i * step[0], y + i * step[1]) for i in range(count)]
        part = jnp.stack(
            [
                jnp.broadcast_to(table[pl.ds(SHARE + first + i * jump, 1), :], (NS, 128))
                for i in range(count)
            ]
        )
        image = flat_zsum(image)
        inv = jnp.stack([inv_ref[a, b] for a, b in spots])
        precond = inv * image
        for i, (a, b) in enumerate(spots):
            v_ref[a, b] = precond[i]
        return acc + jnp.sum(image * precond * part, axis=0), precond

    def with_edges(field, stage, x, y, step, count):
        spots = [(x + i * step[0], y + i * step[1]) for i in range(count)]
        return jnp.stack([field[a, b] + arrived(stage, a, b) for a, b in spots])

    for x in range(8):
        divergence(x)
    store_div = pltpu.make_async_copy(divout_ref, div_out, store_sem.at[0])
    store_div.start()

    def z_stiff(values, weights):
        flat = values.reshape(-1, 128)
        back = slope_product(slope_product(flat, 0) * weights.reshape(-1, 128), 1)
        return back.reshape(values.shape)

    def begin_inside(i, acc):
        planes = []
        for j in range(2):
            x = 1 + 2 * i + j
            acc, precond = begin(x, 1, (0, 1), 6, mp_ref[x, 1:7], my_ref[x, 1:7], acc)
            planes.append(precond)
        first = 1 + 2 * i
        weights = jnp.concatenate([wb_ref[first, 1:7], wb_ref[first + 1, 1:7]], axis=0)
        back = z_stiff(jnp.concatenate(planes, axis=0), weights)
        y_ref[first, 1:7] = back[0:6]
        y_ref[first + 1, 1:7] = back[6:12]
        return acc

    def edge_spots():
        return [(x + i * step[0], y + i * step[1]) for x, y, step, count in EDGES for i in range(count)]

    dot_a = lax.fori_loop(0, 3, begin_inside, none)
    await_from(0, range(8))
    await_from(1, range(8))
    values = []
    for x, y, step, count in EDGES:
        made = with_edges(mp_ref, 1, x, y, step, count)
        carried = with_edges(my_ref, 0, x, y, step, count)
        dot_a, precond = begin(x, y, step, count, made, carried, dot_a)
        values.append(precond)
    weights = jnp.stack([wb_ref[x, y] for x, y in edge_spots()])
    back = z_stiff(jnp.concatenate(values, axis=0), weights)
    for i, (x, y) in enumerate(edge_spots()):
        y_ref[x, y] = back[i]

    def y_lines(plane, weight):
        return jnp.stack(stiff_line([plane[y] for y in range(8)], [weight[y] for y in range(8)]))

    def operate(source, faces_done):
        for x in (0, 7):
            y_ref[x] = y_ref[x] + y_lines(source[x], wb_ref[x])

        def x_part(y, acc):
            values = [source[x, y] for x in range(8)]
            got = stiff_line(values, [wb_ref[x, y] for x in range(8)])
            for x in range(1, 7):
                y_ref[x, y] = y_ref[x, y] + got[x]
            for x in (0, 7):
                image = diff * (y_ref[x, y] + got[x]) + hm_ref[x, y] * values[x]
                y_ref[x, y] = image
                acc = acc + values[x] * image
            return acc

        total = lax.fori_loop(0, 8, x_part, none)
        faces_done()

        def rest_part(i, acc):
            for j in range(2):
                x = 1 + 2 * i + j
                plane = source[x]
                image = diff * (y_ref[x] + y_lines(plane, wb_ref[x])) + hm_ref[x] * plane
                y_ref[x] = image
                acc = acc + jnp.sum(plane * image, axis=0)
            return acc

        return lax.fori_loop(0, 3, rest_part, total)

    def send_faces():
        for d in (0, 1, 4, 5, 6, 7):
            send(2, d, y_ref)

    dot_c = operate(z_ref, send_faces)
    for d in (2, 3):
        send(2, d, y_ref)

    def z_square(values, weights):
        slope = slope_product(values.reshape(-1, 128), 0).reshape(values.shape)
        return jnp.sum(weights * slope * slope, axis=0)

    def advance_inside(i, accs):
        acc, stiff = accs
        planes = []
        for j in range(2):
            x = 1 + 2 * i + j
            acc, precond = advance(x, 1, (0, 1), 6, y_ref[x, 1:7], acc)
            planes.append(precond)
        first = 1 + 2 * i
        weights = jnp.concatenate([wb_ref[first, 1:7], wb_ref[first + 1, 1:7]], axis=0)
        return acc, stiff + z_square(jnp.concatenate(planes, axis=0), weights)

    dot_b, stiff = lax.fori_loop(0, 3, advance_inside, (none, none))
    await_from(2, (2, 3))
    values = []
    for x, y, step, count in EDGES:
        if x == 0:
            await_from(2, (0, 1, 4, 5, 6, 7))
        dot_b, precond = advance(x, y, step, count, with_edges(y_ref, 2, x, y, step, count), dot_b)
        values.append(precond)
    weights = jnp.stack([wb_ref[x, y] for x, y in edge_spots()])
    stiff = stiff + z_square(jnp.concatenate(values, axis=0), weights)

    def square_x(y, acc):
        slopes_x = apply_line([v_ref[x, y] for x in range(8)], FORWARD)
        return acc + sum(wb_ref[x, y] * slopes_x[x] * slopes_x[x] for x in range(8))

    def square_y(i, accs):
        acc, mass = accs
        for j in range(2):
            plane, weight = v_ref[2 * i + j], wb_ref[2 * i + j]
            slope_y = jnp.stack(apply_line([plane[y] for y in range(8)], FORWARD))
            acc = acc + jnp.sum(weight * slope_y * slope_y, axis=0)
            mass = mass + jnp.sum(hm_ref[2 * i + j] * plane * plane, axis=0)
        return acc, mass

    stiff, mass = lax.fori_loop(0, 4, square_y, (stiff, none))
    stiff = lax.fori_loop(0, 8, square_x, stiff)
    dot_d = diff * stiff + mass

    packed = none
    for q, acc in enumerate((dot_a, dot_c, dot_b, dot_d)):
        packed = packed + jnp.where(lane == 16 * q + sub, jnp.sum(acc, axis=1, keepdims=True), 0.0)
    row = jnp.sum(packed, axis=0, keepdims=True)

    def reorder(x, carry):
        for y in range(8):
            where = pl.ds(8 * x + y, NS, stride=XY)
            zt_ref[where, :] = z_ref[x, y]
            vt_ref[where, :] = v_ref[x, y]
        return carry

    store_z = pltpu.make_async_copy(zt_ref, zt_out, store_sem.at[1])
    store_v = pltpu.make_async_copy(vt_ref, vt_out, store_sem.at[2])
    rows_sent = []
    slot = 0
    for phase, (count, peer) in enumerate(((ng, peer_g), (nz, peer_z), (ny, peer_y))):
        srow[phase] = row
        copies = []
        for k in sorted(range(1, count), key=lambda k: -min(k, count - k)):
            copy = pltpu.make_async_remote_copy(
                src_ref=srow.at[phase],
                dst_ref=rrow.at[slot],
                send_sem=row_send.at[slot],
                recv_sem=row_recv.at[slot],
                device_id=peer(k),
                device_id_type=MESH,
            )
            copy.start()
            copies.append((slot, copy))
            slot += 1
        if phase == 0:
            lax.fori_loop(0, 8, reorder, 0)
            store_z.start()
            store_v.start()
        for _, copy in copies:
            copy.wait_recv()
        for at, _ in copies:
            row = row + rrow[at]
        rows_sent += [copy for _, copy in copies]

    totals = jnp.broadcast_to(row, (NS, 128))
    a, c, b, d = [
        jnp.sum(jnp.where(lane == 16 * q + sub, totals, 0.0), axis=1, keepdims=True) for q in range(4)
    ]
    ratio = b / c
    gamma = (c - ratio * a) / (d - ratio * b)
    alpha = a / c - gamma * ratio
    alpha_ref[...] = jnp.broadcast_to(alpha, (NS, 128))
    gamma_ref[...] = jnp.broadcast_to(gamma, (NS, 128))

    for _, _, copy in started:
        copy.wait_send()
    for copy in rows_sent:
        copy.wait_send()
    store_div.wait()
    store_z.wait()
    store_v.wait()


def combine(zt, vt, alpha, gamma, div, out, div_out, *scratch):
    z_ref, v_ref, o_ref, a_ref, g_ref, d_ref, in_sem, out_sem = scratch
    small = [
        pltpu.make_async_copy(alpha, a_ref, in_sem.at[8]),
        pltpu.make_async_copy(gamma, g_ref, in_sem.at[9]),
        pltpu.make_async_copy(div, d_ref, in_sem.at[10]),
    ]
    for one in small:
        one.start()
    parts = [slice(256 * i, 256 * i + 256) for i in range(4)]
    come = []
    for i, part in enumerate(parts):
        come.append(
            (
                pltpu.make_async_copy(zt.at[part], z_ref.at[part], in_sem.at[2 * i]),
                pltpu.make_async_copy(vt.at[part], v_ref.at[part], in_sem.at[2 * i + 1]),
            )
        )
        for one in come[i]:
            one.start()
    for one in small:
        one.wait()
    leave = [pltpu.make_async_copy(d_ref, div_out, out_sem.at[4])]
    leave[0].start()
    for i, part in enumerate(parts):
        for one in come[i]:
            one.wait()
        for j in range(4):
            s = 4 * i + j
            here = slice(XY * s, XY * s + XY)
            o_ref[here, :] = a_ref[s : s + 1, :] * z_ref[here, :] + g_ref[s : s + 1, :] * v_ref[here, :]
        leave.append(pltpu.make_async_copy(o_ref.at[part], out.at[part], out_sem.at[i]))
        leave[-1].start()
    for one in leave:
        one.wait()


def shards(nz, ny, ng, *args):
    share, heat, cond, diff, helm, expn, loga, ea, kin, chg = args
    count = (ng - 1) + (ny - 1) + (nz - 1)
    operands = [
        share.reshape(32 * XY, 128),
        heat.reshape(XY, 128),
        cond.reshape(XY, 128),
        diff.reshape(1, NS),
        helm.reshape(1, NS),
        expn.reshape(1, 32),
        loga.reshape(1, 128),
        ea.reshape(1, 128),
        kin.T,
        chg,
        jnp.asarray(constant_table()),
        jnp.asarray(slope_table()),
    ]
    cube = pltpu.VMEM((8, 8, NS, 128), F32)
    zt, vt, div, alpha, gamma = pl.pallas_call(
        functools.partial(kernel, nz, ny, ng),
        out_shape=(
            jax.ShapeDtypeStruct((NS * XY, 128), F32),
            jax.ShapeDtypeStruct((NS * XY, 128), F32),
            jax.ShapeDtypeStruct((XY, 128), F32),
            jax.ShapeDtypeStruct((NS, 128), F32),
            jax.ShapeDtypeStruct((NS, 128), F32),
        ),
        in_specs=[pl.BlockSpec(memory_space=pltpu.HBM)] * 12,
        out_specs=(
            pl.BlockSpec(memory_space=pltpu.HBM),
            pl.BlockSpec(memory_space=pltpu.HBM),
            pl.BlockSpec(memory_space=pltpu.HBM),
            pl.BlockSpec(memory_space=pltpu.VMEM),
            pl.BlockSpec(memory_space=pltpu.VMEM),
        ),
        scratch_shapes=[pltpu.VMEM(o.shape, o.dtype) for o in operands]
        + [
            pltpu.VMEM((128, 128), BF16),
            pltpu.VMEM((32, 256), BF16),
            pltpu.VMEM((4, XY, 128), F32),
            pltpu.VMEM((XY, 128), F32),
            pltpu.VMEM((XY, 128), F32),
            pltpu.VMEM((XY, 128), F32),
        ]
        + [cube] * 8
        + [
            pltpu.VMEM((3, 4, 8, NS, 128), F32),
            pltpu.VMEM((3, 4, NS, 128), F32),
            pltpu.VMEM((8, NS, 128), F32),
            pltpu.VMEM((8, NS, 128), F32),
            pltpu.VMEM((XY, 128), F32),
            pltpu.VMEM((NS * XY, 128), F32),
            pltpu.VMEM((NS * XY, 128), F32),
            pltpu.VMEM((3, 1, 128), F32),
            pltpu.VMEM((count, 1, 128), F32),
            pltpu.SemaphoreType.DMA((12,)),
            pltpu.SemaphoreType.DMA((3,)),
            pltpu.SemaphoreType.DMA((32,)),
            pltpu.SemaphoreType.DMA((32,)),
            pltpu.SemaphoreType.DMA((count,)),
            pltpu.SemaphoreType.DMA((count,)),
        ],
        compiler_params=pltpu.CompilerParams(
            collective_id=0, has_side_effects=True, vmem_limit_bytes=67043328
        ),
        name="reacting_step",
    )(*operands)
    whole = pltpu.VMEM((NS * XY, 128), F32)
    out, div = pl.pallas_call(
        combine,
        out_shape=(
            jax.ShapeDtypeStruct((NS * XY, 128), F32),
            jax.ShapeDtypeStruct((XY, 128), F32),
        ),
        in_specs=[pl.BlockSpec(memory_space=pltpu.HBM)] * 5,
        out_specs=(
            pl.BlockSpec(memory_space=pltpu.HBM),
            pl.BlockSpec(memory_space=pltpu.HBM),
        ),
        scratch_shapes=[
            whole,
            whole,
            whole,
            pltpu.VMEM((NS, 128), F32),
            pltpu.VMEM((NS, 128), F32),
            pltpu.VMEM((XY, 128), F32),
            pltpu.SemaphoreType.DMA((11,)),
            pltpu.SemaphoreType.DMA((5,)),
        ],
        compiler_params=pltpu.CompilerParams(vmem_limit_bytes=67043328),
        name="combine",
    )(zt, vt, alpha, gamma, div)
    return out.reshape(NS, 8, 8, 128), div.reshape(8, 8, 128)


def solution(mesh):
    ng = mesh.shape["gy"]
    ny = mesh.shape["gx"] // NZ
    field = P("gx", "gy", None)
    species = P(None, "gx", "gy", None)
    return jax.shard_map(
        functools.partial(shards, NZ, ny, ng),
        mesh=mesh,
        in_specs=(species, field, field, P(), P(), P(), P(), P(), P(), P()),
        out_specs=(species, field),
        check_vma=False,
    )
```
